128 devices in a mesh: ctx: 16 (over x, y), fsdp: 8 (over z, core).
Axes of the slice: x: 4, y: 4, z: 4, core: 2. Of those that a mesh axis runs over, the one named last changes fastest.
Arguments:
- tokens: bfloat16 [16384, 4096], P(('ctx', 'fsdp')), may hold values from -360 to 360
- norm_gain: float32 [4096], replicated, may hold values from 0.1 to 1.9
- qkv_weight: bfloat16 [3, 4096, 2048], P(None, 'ctx', 'fsdp'), may hold values from -1 to 1
- out_weight: bfloat16 [2048, 4096], P('fsdp', 'ctx'), may hold values from -1 to 1
- layout: int32 [128, 16], replicated, may hold values from 0 to 127, as said below
Outputs:
- branch_out: bfloat16 [16384, 4096], P(('ctx', 'fsdp'))
The draws below stay inside these ranges and needn't reach their ends.
Inputs may be any that keep to these rules, and one draw needn't show every extreme that they name: `layout`: every entry of query block i names a block of 0 to i. With the blocks taken in spans of 8, the query blocks of one span name at most 2 distinct blocks of any other span, and some pair of spans reaches 2 in every draw.
All inputs are finite; a program needn't handle non-finite values.
Results may differ from the reference program's by a relative error of at most 0.015.
Values may be sent and summed in bfloat16 or wider, within the bound.
A program may use at most 128 MiB of HBM per device.

```python
import math
import jax
import jax.numpy as jnp
from jax import lax

D = 4096
HEADS = 16
HEAD_DIM = 128
BLK = 128
SUMMARY = 16
CAP = 2
INNER = 2048
HEADS_DEV = 2
TOKENS = 16384
BLOCKS = 128
SPAN_BLOCKS = 8


def draw_tokens(key, part):
    subkeys = jax.random.split(key, 3)
    standard = jax.random.truncated_normal(subkeys[0], -3.0, 3.0, (TOKENS, D), jnp.float32)
    row_scale = jnp.exp(jax.random.uniform(subkeys[1], (TOKENS, 1), jnp.float32, 0.0, math.log(10.0)))
    column_scale = jnp.exp(jax.random.uniform(subkeys[2], (1, D), jnp.float32, 0.0, math.log(10.0)))
    return (standard * row_scale * column_scale).astype(jnp.bfloat16)


def draw_qkv_weight(key, part):
    subkeys = jax.random.split(key, 1)
    standard = jax.random.truncated_normal(subkeys[0], -4.0, 4.0, (3, D, INNER), jnp.float32) * D ** (-0.5)
    return standard.astype(jnp.bfloat16)


def draw_layout(key, part):
    subkeys = jax.random.split(key, 5)
    span_count = BLOCKS // SPAN_BLOCKS
    row_ids = jnp.arange(BLOCKS, dtype=jnp.int32)
    home_span = row_ids // SPAN_BLOCKS
    spread = jax.random.randint(subkeys[0], (span_count, span_count, SPAN_BLOCKS), 0, 1 << 20) * SPAN_BLOCKS + jnp.arange(SPAN_BLOCKS, dtype=jnp.int32)
    chosen = jnp.argsort(spread, axis=-1)[..., :CAP].astype(jnp.int32)
    source_span = jax.random.randint(subkeys[1], (BLOCKS, SUMMARY), 0, 1 << 20) % (home_span[:, None] + 1)
    pick_slot = jax.random.randint(subkeys[2], (BLOCKS, SUMMARY), 0, CAP)
    within = jax.random.randint(subkeys[3], (BLOCKS, SUMMARY), 0, 1 << 20) % (row_ids - home_span * SPAN_BLOCKS + 1)[:, None]
    remote = source_span * SPAN_BLOCKS + chosen[home_span[:, None], source_span, pick_slot]
    local_entry = home_span[:, None] * SPAN_BLOCKS + within
    entries = jnp.where(source_span == home_span[:, None], local_entry, remote)
    span_ids = jnp.arange(span_count, dtype=jnp.int32)
    forced_source = jax.random.randint(subkeys[4], (span_count,), 0, 1 << 20) % jnp.maximum(span_ids, 1)
    column_id = jnp.arange(SUMMARY, dtype=jnp.int32)
    forced = forced_source[:, None] * SPAN_BLOCKS + chosen[span_ids[:, None], forced_source[:, None], jnp.minimum(column_id, CAP - 1)[None, :]]
    override = (column_id[None, :] < CAP) & (span_ids[:, None] >= 1)
    first_rows = span_ids * SPAN_BLOCKS
    head_rows = entries[first_rows]
    entries = entries.at[first_rows].set(jnp.where(override, forced, head_rows))
    return entries.astype(jnp.int32)


def shard_levels(key, dims, shards, low, high):
    level = 1.0
    for axis_at, parts in shards:
        draws = jax.random.uniform(jax.random.fold_in(jax.random.fold_in(key, 6), axis_at), (parts,), jnp.float32, low / len(shards), high / len(shards))
        level = level * jnp.repeat(jnp.exp(draws), dims[axis_at] // parts).reshape((-1,) + (1,) * (len(dims) - 1 - axis_at))
    return level


def bell_draw(stream_key, shape, deviation, reach, cuts=(), held_as=jnp.bfloat16):
    drawn = jax.random.normal(stream_key, shape, jnp.float32) * deviation
    if len(cuts) > 0:
        drawn = shard_levels(stream_key, shape, cuts, -0.22, 0.18) * drawn
    return jnp.clip(drawn, min=-reach, max=reach).astype(held_as)


def setup_inputs(seed: int = 0) -> dict:
    key_of = jax.random.split(jax.random.key(seed), 6)
    return {
        "tokens": draw_tokens(jax.random.fold_in(key_of[5], 71), 0),
        "norm_gain": jnp.clip(1.0 + 0.18 * jax.random.normal(key_of[1], (D,), jnp.float32), 0.1, 1.9),
        "qkv_weight": draw_qkv_weight(jax.random.fold_in(key_of[5], 71), 0),
        "out_weight": bell_draw(key_of[3], (INNER, D), (INNER // 64) ** -0.5, 1.0, ((0, 8), (1, 16))),
        "layout": draw_layout(jax.random.fold_in(key_of[5], 71), 0),
    }


EPSILON = 1e-05

def normalize(tokens, norm_gain):
    features = tokens.astype(jnp.float32)
    mean_square = lax.optimization_barrier(jnp.mean(features * features, axis=-1, keepdims=True))
    return (features * lax.rsqrt(mean_square + EPSILON) * norm_gain).astype(jnp.bfloat16)

def reference(tokens, norm_gain, qkv_weight, out_weight, layout):
    normed = normalize(tokens, norm_gain)
    queries = lax.optimization_barrier(jnp.dot(normed, qkv_weight[0], preferred_element_type=jnp.float32).astype(jnp.bfloat16))
    key_rows = lax.optimization_barrier(jnp.dot(normed, qkv_weight[1], preferred_element_type=jnp.float32).astype(jnp.bfloat16))
    value_rows = lax.optimization_barrier(jnp.dot(normed, qkv_weight[2], preferred_element_type=jnp.float32).astype(jnp.bfloat16))
    block_count = TOKENS // BLK
    query_blocks = queries.reshape(block_count, BLK, INNER)
    key_blocks = key_rows.reshape(block_count, BLK, INNER)
    value_blocks = value_rows.reshape(block_count, BLK, INNER)
    key_slots = 2 + SUMMARY

    def one_block(block_id):
        block_id = block_id.astype(jnp.int32)
        key_index = jnp.concatenate([jnp.stack([block_id, block_id - 1]), layout[block_id]]).astype(jnp.int32)
        clipped = jnp.maximum(key_index, 0)
        slot_keys = key_blocks[clipped].astype(jnp.float32).reshape(key_slots, BLK, HEADS, HEAD_DIM)
        slot_values = value_blocks[clipped].astype(jnp.float32).reshape(key_slots, BLK, HEADS, HEAD_DIM)
        block_queries = query_blocks[block_id].astype(jnp.float32).reshape(BLK, HEADS, HEAD_DIM)
        scores = jnp.einsum('qhd,nkhd->hqnk', block_queries, slot_keys) * HEAD_DIM ** (-0.5)
        query_pos = block_id * BLK + jnp.arange(BLK, dtype=jnp.int32)
        key_pos = key_index[:, None] * BLK + jnp.arange(BLK, dtype=jnp.int32)[None, :]
        allowed = (key_pos[None, :, :] <= query_pos[:, None, None]) & (key_pos[None, :, :] >= 0)
        allowed = allowed[None]
        scores = jnp.where(allowed, scores, -1e+30)
        row_max = lax.optimization_barrier(jnp.max(scores, axis=(2, 3), keepdims=True))
        weights = jnp.where(allowed, jnp.exp(scores - row_max), 0.0)
        denominator = lax.optimization_barrier(jnp.sum(weights, axis=(2, 3), keepdims=True))
        weights = lax.optimization_barrier((weights / denominator).astype(jnp.bfloat16)).astype(jnp.float32)
        blended = jnp.einsum('hqnk,nkhd->qhd', weights, slot_values)
        return blended.reshape(BLK, INNER).astype(jnp.bfloat16)
    attended = lax.map(one_block, jnp.arange(block_count, dtype=jnp.int32)).reshape(TOKENS, INNER)
    span_width = HEADS_DEV * HEAD_DIM
    running = jnp.zeros((TOKENS, D), jnp.float32)
    for group_id in range(HEADS // HEADS_DEV):
        part_out = jnp.dot(attended[:, group_id * span_width:(group_id + 1) * span_width], out_weight[group_id * span_width:(group_id + 1) * span_width], preferred_element_type=jnp.float32)
        running = running + lax.optimization_barrier(part_out.astype(jnp.bfloat16)).astype(jnp.float32)
    return running.astype(jnp.bfloat16)
```

```python
import functools

import jax
import jax.numpy as jnp
from jax import lax
from jax.experimental import pallas as pl
from jax.experimental.pallas import tpu as pltpu
from jax.sharding import PartitionSpec as P

HEAD_DIM = 128
BLK = 128
EPSILON = 1e-05
CAP = 2
MESH = pl.DeviceIdType.MESH


def normalize(tokens, norm_gain):
    features = tokens.astype(jnp.float32)
    mean_square = jnp.mean(features * features, axis=-1, keepdims=True)
    return (features * lax.rsqrt(mean_square + EPSILON) * norm_gain).astype(jnp.bfloat16)


def block_tables(layout, spans):
    me = lax.axis_index("ctx")
    blocks, listed = layout.shape
    own = blocks // spans
    entries = layout.reshape(spans, own * listed)
    home, within = entries // own, entries % own
    mine = home == me
    lowest = jnp.min(jnp.where(mine, within, own - 1), axis=1)
    highest = jnp.max(jnp.where(mine, within, 0), axis=1)
    pick = jnp.stack([lowest, highest], axis=1).reshape(-1)
    rows = lax.dynamic_index_in_dim(entries, me, 0, keepdims=False)
    row_home, row_within = rows // own, rows % own
    same = row_home[:, None] == row_home[None, :]
    low = jnp.min(jnp.where(same, row_within[None, :], own - 1), axis=1)
    far = own + CAP * row_home + jnp.where(row_within == low, 0, 1)
    listed_slot = jnp.where(row_home == me, row_within, far).reshape(own, listed)
    index = jnp.arange(own, dtype=jnp.int32)
    block = me * own + index
    before = jnp.where(index > 0, index - 1, jnp.where(me > 0, own + CAP * spans, 0))
    slot = jnp.concatenate([index[:, None], before[:, None], listed_slot], axis=1)
    gap = block[:, None] - rows.reshape(own, listed)
    before_gap = jnp.where(block > 0, 1, -1)
    reach = jnp.concatenate([jnp.zeros_like(index)[:, None], before_gap[:, None], gap], axis=1) * BLK
    return pick.astype(jnp.int32), slot.reshape(-1).astype(jnp.int32), reach.reshape(-1).astype(jnp.int32)


def attend_kernel(
    spans, slots, pick, slot, reach, q, k, v, out, kpool, vpool, kstage, vstage, scores, own_sem, send_sem, recv_sem
):
    me, lane = lax.axis_index("ctx"), lax.axis_index("fsdp")
    own = q.shape[0]
    heads = q.shape[2] // HEAD_DIM
    barrier = pltpu.get_barrier_semaphore()

    @pl.loop(1, spans)
    def _(step):
        peer = lax.rem(me + step, spans)
        pl.semaphore_signal(barrier, inc=1, device_id=(peer, lane), device_id_type=MESH)

    keep = [
        pltpu.make_async_copy(k, kpool.at[pl.ds(0, own)], own_sem.at[0]),
        pltpu.make_async_copy(v, vpool.at[pl.ds(0, own)], own_sem.at[1]),
    ]
    for copy in keep:
        copy.start()

    @pl.loop(0, spans * CAP)
    def _(n):
        kstage[n] = k[pick[n]]
        vstage[n] = v[pick[n]]

    pl.semaphore_wait(barrier, spans - 1)

    def listed(src, dst):
        there = pl.ds(own + CAP * src, CAP)
        return [
            pltpu.make_async_remote_copy(
                stage.at[pl.ds(CAP * dst, CAP)], pool.at[there],
                send_sem.at[dst, j], recv_sem.at[src, j], device_id=(dst, lane), device_id_type=MESH,
            )
            for j, (stage, pool) in enumerate(((kstage, kpool), (vstage, vpool)))
        ]

    def previous(dst):
        there = own + CAP * spans
        return [
            pltpu.make_async_remote_copy(
                mine.at[own - 1], pool.at[there],
                send_sem.at[spans, j], recv_sem.at[spans, j], device_id=(dst, lane), device_id_type=MESH,
            )
            for j, (mine, pool) in enumerate(((k, kpool), (v, vpool)))
        ]

    @pl.when(me < spans - 1)
    def _():
        for copy in previous(me + 1):
            copy.start()

    @pl.loop(1, spans)
    def _(step):
        @pl.when(me + step < spans)
        def _():
            for copy in listed(me, me + step):
                copy.start()

    for copy in keep:
        copy.wait()

    @pl.when(me > 0)
    def _():
        for copy in previous(me):
            copy.wait_recv()

    @pl.loop(1, spans)
    def _(step):
        @pl.when(me >= step)
        def _():
            for copy in listed(me - step, me):
                copy.wait_recv()

    offset = lax.broadcasted_iota(jnp.int32, (BLK, BLK), 1) - lax.broadcasted_iota(jnp.int32, (BLK, BLK), 0)

    @pl.loop(0, own)
    def _(b):
        for head in range(heads):
            columns = pl.ds(head * HEAD_DIM, HEAD_DIM)
            query = q[b, :, columns]
            top = jnp.full((BLK, BLK), -1e30, jnp.float32)
            for n in range(slots):
                keys = kpool[slot[b * slots + n], :, columns]
                part = lax.dot_general(query, keys, (((1,), (1,)), ((), ())), preferred_element_type=jnp.float32)
                part = jnp.where(offset <= reach[b * slots + n], part * HEAD_DIM**-0.5, -1e30)
                scores[n] = part
                top = jnp.maximum(top, part)
            top = jnp.max(top, axis=1, keepdims=True)
            total = jnp.zeros((BLK, BLK), jnp.float32)
            blended = jnp.zeros((BLK, HEAD_DIM), jnp.float32)
            for n in range(slots):
                weights = jnp.exp(scores[n] - top)
                total += weights
                values = vpool[slot[b * slots + n], :, columns]
                blended += jnp.dot(weights.astype(jnp.bfloat16), values, preferred_element_type=jnp.float32)
            total = jnp.sum(total, axis=1, keepdims=True)
            out[b, :, columns] = (blended / total).astype(jnp.bfloat16)

    @pl.when(me < spans - 1)
    def _():
        for copy in previous(me + 1):
            copy.wait_send()

    @pl.loop(1, spans)
    def _(step):
        @pl.when(me + step < spans)
        def _():
            for copy in listed(me, me + step):
                copy.wait_send()


def exchange_and_attend(q, k, v, layout, spans):
    rows, width = q.shape
    slots = 2 + layout.shape[1]
    pick, slot, reach = block_tables(layout, spans)
    own = rows // BLK
    pool = own + CAP * spans + 1
    q, k, v = (each.reshape(own, BLK, width) for each in (q, k, v))
    smem = pl.BlockSpec(memory_space=pltpu.SMEM)
    vmem = pl.BlockSpec(memory_space=pltpu.VMEM)
    return pl.pallas_call(
        functools.partial(attend_kernel, spans, slots),
        out_shape=jax.ShapeDtypeStruct((own, BLK, width), jnp.bfloat16),
        in_specs=[smem] * 3 + [vmem] * 3,
        out_specs=vmem,
        scratch_shapes=[
            pltpu.VMEM((pool, BLK, width), jnp.bfloat16),
            pltpu.VMEM((pool, BLK, width), jnp.bfloat16),
            pltpu.VMEM((spans * CAP, BLK, width), jnp.bfloat16),
            pltpu.VMEM((spans * CAP, BLK, width), jnp.bfloat16),
            pltpu.VMEM((slots, BLK, BLK), jnp.float32),
            pltpu.SemaphoreType.DMA((2,)),
            pltpu.SemaphoreType.DMA((spans + 1, 2)),
            pltpu.SemaphoreType.DMA((spans + 1, 2)),
        ],
        compiler_params=pltpu.CompilerParams(
            collective_id=0, has_side_effects=True, vmem_limit_bytes=48 * 2**20
        ),
    )(pick, slot, reach, q, k, v).reshape(rows, width)


def shards(spans, tokens, norm_gain, qkv_weight, out_weight, layout):
    normed = normalize(tokens, norm_gain)
    gathered = lax.all_gather(normed, "fsdp", axis=0, tiled=True)
    projected = jnp.einsum(
        "td,cdi->cti",
        gathered,
        lax.all_gather(qkv_weight, "ctx", axis=1, tiled=True),
        preferred_element_type=jnp.float32,
    ).astype(jnp.bfloat16)
    attended = exchange_and_attend(projected[0], projected[1], projected[2], layout, spans)
    projection = lax.all_gather(out_weight, "ctx", axis=1, tiled=True)
    return lax.psum_scatter(
        jnp.dot(attended, projection, preferred_element_type=jnp.float32).astype(jnp.bfloat16),
        "fsdp",
        scatter_dimension=0,
        tiled=True,
    )


def solution(mesh):
    placed = (P(("ctx", "fsdp"), None), P(), P(None, "ctx", "fsdp"), P("fsdp", "ctx"), P())
    return jax.shard_map(
        functools.partial(shards, mesh.shape["ctx"]),
        mesh=mesh, in_specs=placed, out_specs=P(("ctx", "fsdp"), None), check_vma=False,
    )
```

```python
import functools
import math

import jax
import jax.numpy as jnp
from jax import lax
from jax.experimental import pallas as pl
from jax.experimental.pallas import tpu as pltpu
from jax.sharding import PartitionSpec as P

HEAD_DIM = 128
BLK = 128
EPSILON = 1e-05
CAP = 2
MESH = pl.DeviceIdType.MESH


def block_tables(layout, spans):
    me = lax.axis_index("ctx")
    blocks, listed = layout.shape
    own = blocks // spans
    entries = layout.reshape(spans, own * listed)
    home, within = entries // own, entries % own
    mine = home == me
    lowest = jnp.min(jnp.where(mine, within, own - 1), axis=1)
    highest = jnp.max(jnp.where(mine, within, 0), axis=1)
    pick = jnp.stack([lowest, highest], axis=1).reshape(-1)
    rows = lax.dynamic_index_in_dim(entries, me, 0, keepdims=False)
    row_home, row_within = rows // own, rows % own
    same = row_home[:, None] == row_home[None, :]
    low = jnp.min(jnp.where(same, row_within[None, :], own - 1), axis=1)
    far = own + CAP * row_home + jnp.where(row_within == low, 0, 1)
    listed_slot = jnp.where(row_home == me, row_within, far).reshape(own, listed)
    index = jnp.arange(own, dtype=jnp.int32)
    block = me * own + index
    before = jnp.where(index > 0, index - 1, jnp.where(me > 0, own + CAP * spans, 0))
    slot = jnp.concatenate([index[:, None], before[:, None], listed_slot], axis=1)
    gap = block[:, None] - rows.reshape(own, listed)
    before_gap = jnp.where(block > 0, 1, -1)
    reach = jnp.concatenate([jnp.zeros_like(index)[:, None], before_gap[:, None], gap], axis=1) * BLK
    return pick.astype(jnp.int32), slot.reshape(-1).astype(jnp.int32), reach.reshape(-1).astype(jnp.int32)


def attend_kernel(
    spans, slots, pick, slot, reach, q, k, v, out, kpool, vpool, kstage, vstage, scores, own_sem, send_sem, recv_sem
):
    me, lane = lax.axis_index("ctx"), lax.axis_index("fsdp")
    own = q.shape[0]
    heads = q.shape[2] // HEAD_DIM
    barrier = pltpu.get_barrier_semaphore()

    @pl.loop(1, spans)
    def _(step):
        peer = lax.rem(me + step, spans)
        pl.semaphore_signal(barrier, inc=1, device_id=(peer, lane), device_id_type=MESH)

    keep = [
        pltpu.make_async_copy(k, kpool.at[pl.ds(0, own)], own_sem.at[0]),
        pltpu.make_async_copy(v, vpool.at[pl.ds(0, own)], own_sem.at[1]),
    ]
    for copy in keep:
        copy.start()

    @pl.loop(0, spans * CAP)
    def _(n):
        kstage[n] = k[pick[n]]
        vstage[n] = v[pick[n]]

    pl.semaphore_wait(barrier, spans - 1)

    def listed(src, dst):
        there = pl.ds(own + CAP * src, CAP)
        return [
            pltpu.make_async_remote_copy(
                stage.at[pl.ds(CAP * dst, CAP)], pool.at[there],
                send_sem.at[dst, j], recv_sem.at[src, j], device_id=(dst, lane), device_id_type=MESH,
            )
            for j, (stage, pool) in enumerate(((kstage, kpool), (vstage, vpool)))
        ]

    def previous(dst):
        there = own + CAP * spans
        return [
            pltpu.make_async_remote_copy(
                mine.at[own - 1], pool.at[there],
                send_sem.at[spans, j], recv_sem.at[spans, j], device_id=(dst, lane), device_id_type=MESH,
            )
            for j, (mine, pool) in enumerate(((k, kpool), (v, vpool)))
        ]

    @pl.when(me < spans - 1)
    def _():
        for copy in previous(me + 1):
            copy.start()

    @pl.loop(1, spans)
    def _(step):
        @pl.when(me + step < spans)
        def _():
            for copy in listed(me, me + step):
                copy.start()

    for copy in keep:
        copy.wait()

    @pl.when(me > 0)
    def _():
        for copy in previous(me):
            copy.wait_recv()

    @pl.loop(1, spans)
    def _(step):
        @pl.when(me >= step)
        def _():
            for copy in listed(me - step, me):
                copy.wait_recv()

    offset = lax.broadcasted_iota(jnp.int32, (BLK, BLK), 1) - lax.broadcasted_iota(jnp.int32, (BLK, BLK), 0)

    @pl.loop(0, own)
    def _(b):
        for head in range(heads):
            columns = pl.ds(head * HEAD_DIM, HEAD_DIM)
            query = q[b, :, columns]
            top = jnp.full((BLK, BLK), -1e30, jnp.float32)
            for n in range(slots):
                keys = kpool[slot[b * slots + n], :, columns]
                part = lax.dot_general(query, keys, (((1,), (1,)), ((), ())), preferred_element_type=jnp.float32)
                part = jnp.where(offset <= reach[b * slots + n], part * HEAD_DIM**-0.5, -1e30)
                scores[n] = part
                top = jnp.maximum(top, part)
            top = jnp.max(top, axis=1, keepdims=True)
            total = jnp.zeros((BLK, BLK), jnp.float32)
            blended = jnp.zeros((BLK, HEAD_DIM), jnp.float32)
            for n in range(slots):
                weights = jnp.exp(scores[n] - top)
                total += weights
                values = vpool[slot[b * slots + n], :, columns]
                blended += jnp.dot(weights.astype(jnp.bfloat16), values, preferred_element_type=jnp.float32)
            total = jnp.sum(total, axis=1, keepdims=True)
            out[b, :, columns] = (blended / total).astype(jnp.bfloat16)

    @pl.when(me < spans - 1)
    def _():
        for copy in previous(me + 1):
            copy.wait_send()

    @pl.loop(1, spans)
    def _(step):
        @pl.when(me + step < spans)
        def _():
            for copy in listed(me, me + step):
                copy.wait_send()


def exchange_and_attend(q, k, v, layout, spans):
    rows, width = q.shape
    slots = 2 + layout.shape[1]
    pick, slot, reach = block_tables(layout, spans)
    own = rows // BLK
    pool = own + CAP * spans + 1
    q, k, v = (each.reshape(own, BLK, width) for each in (q, k, v))
    smem = pl.BlockSpec(memory_space=pltpu.SMEM)
    vmem = pl.BlockSpec(memory_space=pltpu.VMEM)
    return pl.pallas_call(
        functools.partial(attend_kernel, spans, slots),
        out_shape=jax.ShapeDtypeStruct((own, BLK, width), jnp.bfloat16),
        in_specs=[smem] * 3 + [vmem] * 3,
        out_specs=vmem,
        scratch_shapes=[
            pltpu.VMEM((pool, BLK, width), jnp.bfloat16),
            pltpu.VMEM((pool, BLK, width), jnp.bfloat16),
            pltpu.VMEM((spans * CAP, BLK, width), jnp.bfloat16),
            pltpu.VMEM((spans * CAP, BLK, width), jnp.bfloat16),
            pltpu.VMEM((slots, BLK, BLK), jnp.float32),
            pltpu.SemaphoreType.DMA((2,)),
            pltpu.SemaphoreType.DMA((spans + 1, 2)),
            pltpu.SemaphoreType.DMA((spans + 1, 2)),
        ],
        compiler_params=pltpu.CompilerParams(
            collective_id=0, has_side_effects=True, vmem_limit_bytes=48 * 2**20
        ),
    )(pick, slot, reach, q, k, v).reshape(rows, width)


def gather_kernel(side, eps, tokens, gain, weights, projected, projection, rows_all, normed, held, send_t, recv_t, send_w, recv_w, own_sem):
    ctx, lane = lax.axis_index("ctx"), lax.axis_index("fsdp")
    x, y = ctx // side, lax.rem(ctx, side)
    z, core = lane // 2, lax.rem(lane, 2)
    part, width = tokens.shape
    depth = weights.shape[1]
    half, quarter = part // 2, depth // 4

    def shift(at, by):
        return lax.rem(at + by + side, side)

    def along(axis, by):
        if axis == "x":
            return (shift(x, by) * side + y, lane)
        if axis == "y":
            return (x * side + shift(y, by), lane)
        if axis == "z":
            return (ctx, shift(z, by) * 2 + core)
        return (ctx, z * 2 + 1 - core)

    barrier = pltpu.get_barrier_semaphore()
    peers = [along(axis, by) for axis in "xyz" for by in (1, -1)] + [along("core", 1)]
    for peer in peers:
        pl.semaphore_signal(barrier, inc=1, device_id=peer, device_id_type=MESH)

    sent = []

    def send_tokens(owner, h, peer, own=False):
        there = rows_all.at[pl.ds(pl.multiple_of(owner * part + h * half, half), half)]
        here = tokens.at[pl.ds(h * half, half)] if own else there
        copy = pltpu.make_async_remote_copy(
            here, there, send_t.at[len([c for c in sent if c[0] == "t"])], recv_t.at[owner, h], device_id=peer, device_id_type=MESH
        )
        copy.start()
        sent.append(("t", copy))

    def wait_tokens(owner, h):
        there = rows_all.at[pl.ds(pl.multiple_of(owner * part + h * half, half), half)]
        pltpu.make_async_remote_copy(
            there, there, send_t.at[0], recv_t.at[owner, h], device_id=along("core", 1), device_id_type=MESH
        ).wait_recv()

    def piece_of(owner, p):
        return held.at[:, pl.ds(pl.multiple_of(owner * depth + p * quarter, quarter), quarter)]

    def send_weights(owner, p, peer, own=False):
        there = piece_of(owner, p)
        here = weights.at[:, pl.ds(p * quarter, quarter)] if own else there
        copy = pltpu.make_async_remote_copy(
            here, there, send_w.at[len([c for c in sent if c[0] == "w"])], recv_w.at[owner, p], device_id=peer, device_id_type=MESH
        )
        copy.start()
        sent.append(("w", copy))

    def wait_weights(owner, p):
        pltpu.make_async_remote_copy(
            piece_of(owner, p), piece_of(owner, p), send_w.at[0], recv_w.at[owner, p], device_id=along("core", 1), device_id_type=MESH
        ).wait_recv()

    def normalize_rows(owner):
        @pl.loop(0, part // 16)
        def _(n):
            at = pl.ds(pl.multiple_of(owner * part + n * 16, 16), 16)
            features = rows_all[at, :].astype(jnp.float32)
            mean_square = jnp.mean(features * features, axis=-1, keepdims=True)
            normed[at, :] = (features * lax.rsqrt(mean_square + eps) * gain[...]).astype(jnp.bfloat16)

    keep = [
        pltpu.make_async_copy(tokens, rows_all.at[pl.ds(pl.multiple_of(lane * part, part), part)], own_sem.at[0]),
        pltpu.make_async_copy(weights, held.at[:, pl.ds(pl.multiple_of(ctx * depth, depth), depth)], own_sem.at[1]),
    ]
    for copy in keep:
        copy.start()
    pl.semaphore_wait(barrier, len(peers))

    routes = (("x", "y", 0), ("y", "x", 2))

    def owner_at(axis, by, other=0):
        if axis == "x":
            return shift(x, by) * side + shift(y, other)
        return shift(x, other) * side + shift(y, by)

    right, left, sibling = along("z", 1), along("z", -1), along("core", 1)
    lane_at = lambda by, flip=0: shift(z, by) * 2 + (1 - core if flip else core)
    send_tokens(lane, 0, right, own=True)
    send_tokens(lane, 1, left, own=True)
    for first, second, p in routes:
        send_weights(ctx, p, along(first, 1), own=True)
        send_weights(ctx, p + 1, along(first, -1), own=True)
        send_weights(ctx, p + 1, along(first, 1), own=True)
        send_weights(ctx, p, along(first, -1), own=True)
    send_tokens(lane, 1, right, own=True)
    send_tokens(lane, 0, left, own=True)
    for h in range(2):
        send_tokens(lane, h, sibling, own=True)
    for first, second, p in routes:
        send_weights(ctx, p, along(second, 1), own=True)
        send_weights(ctx, p + 1, along(second, -1), own=True)
        send_weights(ctx, p + 1, along(second, 1), own=True)
        send_weights(ctx, p, along(second, -1), own=True)
    for copy in keep:
        copy.wait()
    normalize_rows(lane)

    def spread(owner, p, axis):
        send_weights(owner, p, along(axis, 1))
        send_weights(owner, p, along(axis, -1))

    for first, second, p in routes:
        wait_weights(owner_at(first, -1), p)
        send_weights(owner_at(first, -1), p, along(first, 1))
        wait_weights(owner_at(first, 1), p + 1)
        send_weights(owner_at(first, 1), p + 1, along(first, -1))
    for first, second, p in routes:
        spread(owner_at(first, -1), p, second)
        spread(owner_at(first, 1), p + 1, second)
    for first, second, p in routes:
        wait_weights(owner_at(first, -1), p + 1)
        spread(owner_at(first, -1), p + 1, second)
        wait_weights(owner_at(first, 1), p)
        spread(owner_at(first, 1), p, second)

    def relay(by):
        for first, second, p in routes:
            owner = owner_at(first, by, -1)
            wait_weights(owner, p)
            send_weights(owner, p, along(second, 1))
            owner = owner_at(first, by, 1)
            wait_weights(owner, p + 1)
            send_weights(owner, p + 1, along(second, -1))

    for first, second, p in routes:
        for q in (p, p + 1):
            wait_weights(owner_at(first, 2), q)
            spread(owner_at(first, 2), q, second)
    relay(0)
    wait_tokens(lane_at(-1), 0)
    send_tokens(lane_at(-1), 0, right)
    send_tokens(lane_at(-1), 0, sibling)
    wait_tokens(lane_at(1), 1)
    send_tokens(lane_at(1), 1, left)
    send_tokens(lane_at(1), 1, sibling)
    relay(-1)
    relay(1)
    for h in range(2):
        wait_tokens(lane_at(0, 1), h)
    normalize_rows(lane_at(0, 1))
    wait_tokens(lane_at(-1), 1)
    send_tokens(lane_at(-1), 1, sibling)
    wait_tokens(lane_at(1), 0)
    send_tokens(lane_at(1), 0, sibling)
    normalize_rows(lane_at(-1))
    normalize_rows(lane_at(1))
    relay(2)
    for by in (-1, 1):
        for h in range(2):
            wait_tokens(lane_at(by, 1), h)
        normalize_rows(lane_at(by, 1))
    for h in range(2):
        wait_tokens(lane_at(2), h)
        send_tokens(lane_at(2), h, sibling)
    normalize_rows(lane_at(2))
    for first, second, p in routes:
        for by in (0, -1, 1, 2):
            wait_weights(owner_at(first, by, -1), p + 1)
            wait_weights(owner_at(first, by, 1), p)
            wait_weights(owner_at(first, by, 2), p)
            wait_weights(owner_at(first, by, 2), p + 1)
    for h in range(2):
        wait_tokens(lane_at(2, 1), h)
    normalize_rows(lane_at(2, 1))

    tile = 256
    steps = normed.shape[0] // tile
    give = pltpu.make_async_copy(held.at[3], projection, own_sem.at[0])
    give.start()

    @pl.loop(0, 3 * steps)
    def _(n):
        which, at = n // steps, pl.ds(pl.multiple_of(lax.rem(n, steps) * tile, tile), tile)
        projected[which, at, :] = jnp.dot(normed[at, :], held[which], preferred_element_type=jnp.float32).astype(jnp.bfloat16)

    give.wait()
    for _, copy in sent:
        copy.wait_send()


def gather_and_project(tokens, norm_gain, qkv_weight, out_weight, side, lanes):
    part, width = tokens.shape
    columns = qkv_weight.shape[2]
    weights = jnp.concatenate([qkv_weight, out_weight[None]], axis=0)
    vmem = pl.BlockSpec(memory_space=pltpu.VMEM)
    return pl.pallas_call(
        functools.partial(gather_kernel, side, EPSILON),
        out_shape=[
            jax.ShapeDtypeStruct((3, lanes * part, columns), jnp.bfloat16),
            jax.ShapeDtypeStruct((width, columns), jnp.bfloat16),
        ],
        in_specs=[vmem] * 3,
        out_specs=[vmem] * 2,
        scratch_shapes=[
            pltpu.VMEM((lanes * part, width), jnp.bfloat16),
            pltpu.VMEM((lanes * part, width), jnp.bfloat16),
            pltpu.VMEM((4, width, columns), jnp.bfloat16),
            pltpu.SemaphoreType.DMA((14,)),
            pltpu.SemaphoreType.DMA((lanes, 2)),
            pltpu.SemaphoreType.DMA((60,)),
            pltpu.SemaphoreType.DMA((side * side, 4)),
            pltpu.SemaphoreType.DMA((2,)),
        ],
        compiler_params=pltpu.CompilerParams(
            collective_id=1, has_side_effects=True, vmem_limit_bytes=60 * 2**20
        ),
    )(tokens, norm_gain[None, :], weights)


def shards(spans, lanes, tokens, norm_gain, qkv_weight, out_weight, layout):
    side = math.isqrt(spans)
    projected, projection = gather_and_project(tokens, norm_gain, qkv_weight, out_weight, side, lanes)
    attended = exchange_and_attend(projected[0], projected[1], projected[2], layout, spans)
    product = jnp.einsum(
        "tk,jkd->tjd", attended, projection.reshape(spans, -1, projection.shape[1]), preferred_element_type=jnp.float32
    ).astype(jnp.bfloat16)
    return lax.psum_scatter(product.reshape(attended.shape[0], -1), "fsdp", scatter_dimension=0, tiled=True)


def solution(mesh):
    placed = (P(("ctx", "fsdp"), None), P(), P(None, "ctx", "fsdp"), P("fsdp", "ctx"), P())
    return jax.shard_map(
        functools.partial(shards, mesh.shape["ctx"], mesh.shape["fsdp"]),
        mesh=mesh, in_specs=placed, out_specs=P(("ctx", "fsdp"), None), check_vma=False,
    )
```

```python
import functools
import math

import jax
import jax.numpy as jnp
from jax import lax
from jax.experimental import pallas as pl
from jax.experimental.pallas import tpu as pltpu
from jax.sharding import PartitionSpec as P

HEAD_DIM = 128
BLK = 128
EPSILON = 1e-05
CAP = 2
MESH = pl.DeviceIdType.MESH


def block_tables(layout, spans):
    me = lax.axis_index("ctx")
    blocks, listed = layout.shape
    own = blocks // spans
    entries = layout.reshape(spans, own * listed)
    home, within = entries // own, entries % own
    mine = home == me
    lowest = jnp.min(jnp.where(mine, within, own - 1), axis=1)
    highest = jnp.max(jnp.where(mine, within, 0), axis=1)
    pick = jnp.stack([lowest, highest], axis=1).reshape(-1)
    rows = lax.dynamic_index_in_dim(entries, me, 0, keepdims=False)
    row_home, row_within = rows // own, rows % own
    same = row_home[:, None] == row_home[None, :]
    low = jnp.min(jnp.where(same, row_within[None, :], own - 1), axis=1)
    far = own + CAP * row_home + jnp.where(row_within == low, 0, 1)
    listed_slot = jnp.where(row_home == me, row_within, far).reshape(own, listed)
    index = jnp.arange(own, dtype=jnp.int32)
    block = me * own + index
    before = jnp.where(index > 0, index - 1, jnp.where(me > 0, own + CAP * spans, 0))
    slot = jnp.concatenate([index[:, None], before[:, None], listed_slot], axis=1)
    gap = block[:, None] - rows.reshape(own, listed)
    before_gap = jnp.where(block > 0, 1, -1)
    reach = jnp.concatenate([jnp.zeros_like(index)[:, None], before_gap[:, None], gap], axis=1) * BLK
    return pick.astype(jnp.int32), slot.reshape(-1).astype(jnp.int32), reach.reshape(-1).astype(jnp.int32)


def attend_kernel(
    spans, slots, pick, slot, reach, q, k, v, projection, out,
    kpool, vpool, kstage, vstage, scores, attended, partial, crossed, packed, hop, final,
    own_sem, send_sem, recv_sem, cross_sem, sum_send, sum_recv,
):
    me, lane = lax.axis_index("ctx"), lax.axis_index("fsdp")
    z, core = lane // 2, lax.rem(lane, 2)
    chips = 4
    pieces = projection.shape[0]
    wide = projection.shape[2]
    half = pieces // 2
    right = (me, lax.rem(z + 1, chips) * 2 + core)
    left = (me, lax.rem(z + chips - 1, chips) * 2 + core)
    sibling = (me, z * 2 + 1 - core)
    own = q.shape[0]
    heads = q.shape[2] // HEAD_DIM
    barrier = pltpu.get_barrier_semaphore()

    @pl.loop(1, spans)
    def _(step):
        peer = lax.rem(me + step, spans)
        pl.semaphore_signal(barrier, inc=1, device_id=(peer, lane), device_id_type=MESH)

    for peer in (right, left, sibling):
        pl.semaphore_signal(barrier, inc=1, device_id=peer, device_id_type=MESH)

    keep = [
        pltpu.make_async_copy(k, kpool.at[pl.ds(0, own)], own_sem.at[0]),
        pltpu.make_async_copy(v, vpool.at[pl.ds(0, own)], own_sem.at[1]),
    ]
    for copy in keep:
        copy.start()

    @pl.loop(0, spans * CAP)
    def _(n):
        kstage[n] = k[pick[n]]
        vstage[n] = v[pick[n]]

    pl.semaphore_wait(barrier, spans + 2)

    def listed(src, dst):
        there = pl.ds(own + CAP * src, CAP)
        return [
            pltpu.make_async_remote_copy(
                stage.at[pl.ds(CAP * dst, CAP)], pool.at[there],
                send_sem.at[dst, j], recv_sem.at[src, j], device_id=(dst, lane), device_id_type=MESH,
            )
            for j, (stage, pool) in enumerate(((kstage, kpool), (vstage, vpool)))
        ]

    def previous(dst):
        there = own + CAP * spans
        return [
            pltpu.make_async_remote_copy(
                mine.at[own - 1], pool.at[there],
                send_sem.at[spans, j], recv_sem.at[spans, j], device_id=(dst, lane), device_id_type=MESH,
            )
            for j, (mine, pool) in enumerate(((k, kpool), (v, vpool)))
        ]

    @pl.when(me < spans - 1)
    def _():
        for copy in previous(me + 1):
            copy.start()

    @pl.loop(1, spans)
    def _(step):
        @pl.when(me + step < spans)
        def _():
            for copy in listed(me, me + step):
                copy.start()

    for copy in keep:
        copy.wait()

    @pl.when(me > 0)
    def _():
        for copy in previous(me):
            copy.wait_recv()

    @pl.loop(1, spans)
    def _(step):
        @pl.when(me >= step)
        def _():
            for copy in listed(me - step, me):
                copy.wait_recv()

    offset = lax.broadcasted_iota(jnp.int32, (BLK, BLK), 1) - lax.broadcasted_iota(jnp.int32, (BLK, BLK), 0)

    def attend(b, at):
        for head in range(heads):
            columns = pl.ds(head * HEAD_DIM, HEAD_DIM)
            query = q[b, :, columns]
            top = jnp.full((BLK, BLK), -1e30, jnp.float32)
            for n in range(slots):
                keys = kpool[slot[b * slots + n], :, columns]
                part = lax.dot_general(query, keys, (((1,), (1,)), ((), ())), preferred_element_type=jnp.float32)
                part = jnp.where(offset <= reach[b * slots + n], part * HEAD_DIM**-0.5, -1e30)
                scores[n] = part
                top = jnp.maximum(top, part)
            top = jnp.max(top, axis=1, keepdims=True)
            total = jnp.zeros((BLK, BLK), jnp.float32)
            blended = jnp.zeros((BLK, HEAD_DIM), jnp.float32)
            for n in range(slots):
                weights = jnp.exp(scores[n] - top)
                total += weights
                values = vpool[slot[b * slots + n], :, columns]
                blended += jnp.dot(weights.astype(jnp.bfloat16), values, preferred_element_type=jnp.float32)
            total = jnp.sum(total, axis=1, keepdims=True)
            attended[at, :, columns] = (blended / total).astype(jnp.bfloat16)

    def cross(g):
        return pltpu.make_async_remote_copy(
            partial.at[g, 0], crossed.at[g], cross_sem.at[0, g], cross_sem.at[1, g], device_id=sibling, device_id_type=MESH
        )

    def travel(n, source, target, peer):
        return pltpu.make_async_remote_copy(
            source, target, sum_send.at[n], sum_recv.at[n], device_id=peer, device_id_type=MESH
        )

    first, second = pl.ds(0, half), pl.ds(half, half)
    travels = [
        travel(0, packed.at[0, first], hop.at[0], right),
        travel(1, packed.at[0, second], hop.at[1], left),
        travel(2, packed.at[1, second], final.at[0, second], right),
        travel(3, packed.at[1, first], final.at[0, first], right),
        travel(4, packed.at[2, first], final.at[1, first], left),
        travel(5, packed.at[2, second], final.at[1, second], left),
    ]

    def add(g, low, more=None):
        @pl.loop(0, half)
        def _(n):
            term = partial[g, 1, low + n].astype(jnp.float32) + crossed[g, low + n].astype(jnp.float32)
            if more is not None:
                term += hop[more, n].astype(jnp.float32)
            packed[g, low + n] = term.astype(jnp.bfloat16)

    for g, steps in enumerate((2, 1, -1, 0)):
        chip = lax.rem(z + steps + chips, chips)

        @pl.loop(0, 2)
        def _(turn):
            attend(chip * 2 + lax.rem(core + 1 + turn, 2), turn)

            @pl.loop(0, pieces)
            def _(n):
                partial[g, turn, n] = jnp.dot(
                    attended[turn], projection[n], preferred_element_type=jnp.float32
                ).astype(jnp.bfloat16)

            @pl.when(turn == 0)
            def _():
                cross(g).start()

        cross(g).wait_recv()
        if g == 0:
            add(0, 0)
            travels[0].start()
            add(0, half)
            travels[1].start()
        elif g == 1:
            add(1, half)
            travels[2].start()
            travels[0].wait_recv()
            add(1, 0, 0)
            travels[3].start()
        elif g == 2:
            add(2, 0)
            travels[4].start()
            travels[1].wait_recv()
            add(2, half, 1)
            travels[5].start()

    for low, waits in ((half, (2, 5)), (0, (3, 4))):
        for n in waits:
            travels[n].wait_recv()

        @pl.loop(0, half)
        def _(n):
            at = low + n
            term = partial[3, 1, at].astype(jnp.float32) + crossed[3, at].astype(jnp.float32)
            term += final[0, at].astype(jnp.float32) + final[1, at].astype(jnp.float32)
            out[:, pl.ds(pl.multiple_of(at * wide, wide), wide)] = term.astype(jnp.bfloat16)

    for g in range(chips):
        cross(g).wait_send()
    for copy in travels:
        copy.wait_send()

    @pl.when(me < spans - 1)
    def _():
        for copy in previous(me + 1):
            copy.wait_send()

    @pl.loop(1, spans)
    def _(step):
        @pl.when(me + step < spans)
        def _():
            for copy in listed(me, me + step):
                copy.wait_send()


def attend_and_reduce(q, k, v, projection, layout, spans):
    rows, width = q.shape
    slots = 2 + layout.shape[1]
    pick, slot, reach = block_tables(layout, spans)
    own = rows // BLK
    pool = own + CAP * spans + 1
    pieces, _, wide = projection.shape
    whole = (pieces, BLK, wide)
    q, k, v = (each.reshape(own, BLK, width) for each in (q, k, v))
    smem = pl.BlockSpec(memory_space=pltpu.SMEM)
    vmem = pl.BlockSpec(memory_space=pltpu.VMEM)
    return pl.pallas_call(
        functools.partial(attend_kernel, spans, slots),
        out_shape=jax.ShapeDtypeStruct((BLK, pieces * wide), jnp.bfloat16),
        in_specs=[smem] * 3 + [vmem] * 4,
        out_specs=vmem,
        scratch_shapes=[
            pltpu.VMEM((pool, BLK, width), jnp.bfloat16),
            pltpu.VMEM((pool, BLK, width), jnp.bfloat16),
            pltpu.VMEM((spans * CAP, BLK, width), jnp.bfloat16),
            pltpu.VMEM((spans * CAP, BLK, width), jnp.bfloat16),
            pltpu.VMEM((slots, BLK, BLK), jnp.float32),
            pltpu.VMEM((2, BLK, width), jnp.bfloat16),
            pltpu.VMEM((4, 2, *whole), jnp.bfloat16),
            pltpu.VMEM((4, *whole), jnp.bfloat16),
            pltpu.VMEM((3, *whole), jnp.bfloat16),
            pltpu.VMEM((2, pieces // 2, BLK, wide), jnp.bfloat16),
            pltpu.VMEM((2, *whole), jnp.bfloat16),
            pltpu.SemaphoreType.DMA((2,)),
            pltpu.SemaphoreType.DMA((spans + 1, 2)),
            pltpu.SemaphoreType.DMA((spans + 1, 2)),
            pltpu.SemaphoreType.DMA((2, 4)),
            pltpu.SemaphoreType.DMA((6,)),
            pltpu.SemaphoreType.DMA((6,)),
        ],
        compiler_params=pltpu.CompilerParams(
            collective_id=0, has_side_effects=True, vmem_limit_bytes=60 * 2**20
        ),
    )(pick, slot, reach, q, k, v, projection)


def gather_kernel(side, eps, tokens, gain, weights, projected, projection, rows_all, normed, held, send_t, recv_t, send_w, recv_w, own_sem):
    ctx, lane = lax.axis_index("ctx"), lax.axis_index("fsdp")
    x, y = ctx // side, lax.rem(ctx, side)
    z, core = lane // 2, lax.rem(lane, 2)
    part, width = tokens.shape
    depth = weights.shape[1]
    half, quarter = part // 2, depth // 4

    def shift(at, by):
        return lax.rem(at + by + side, side)

    def along(axis, by):
        if axis == "x":
            return (shift(x, by) * side + y, lane)
        if axis == "y":
            return (x * side + shift(y, by), lane)
        if axis == "z":
            return (ctx, shift(z, by) * 2 + core)
        return (ctx, z * 2 + 1 - core)

    barrier = pltpu.get_barrier_semaphore()
    peers = [along(axis, by) for axis in "xyz" for by in (1, -1)] + [along("core", 1)]
    for peer in peers:
        pl.semaphore_signal(barrier, inc=1, device_id=peer, device_id_type=MESH)

    sent = []

    def send_tokens(owner, h, peer, own=False):
        there = rows_all.at[pl.ds(pl.multiple_of(owner * part + h * half, half), half)]
        here = tokens.at[pl.ds(h * half, half)] if own else there
        copy = pltpu.make_async_remote_copy(
            here, there, send_t.at[len([c for c in sent if c[0] == "t"])], recv_t.at[owner, h], device_id=peer, device_id_type=MESH
        )
        copy.start()
        sent.append(("t", copy))

    def wait_tokens(owner, h):
        there = rows_all.at[pl.ds(pl.multiple_of(owner * part + h * half, half), half)]
        pltpu.make_async_remote_copy(
            there, there, send_t.at[0], recv_t.at[owner, h], device_id=along("core", 1), device_id_type=MESH
        ).wait_recv()

    def piece_of(owner, p):
        return held.at[:, pl.ds(pl.multiple_of(owner * depth + p * quarter, quarter), quarter)]

    def send_weights(owner, p, peer, own=False):
        there = piece_of(owner, p)
        here = weights.at[:, pl.ds(p * quarter, quarter)] if own else there
        copy = pltpu.make_async_remote_copy(
            here, there, send_w.at[len([c for c in sent if c[0] == "w"])], recv_w.at[owner, p], device_id=peer, device_id_type=MESH
        )
        copy.start()
        sent.append(("w", copy))

    def wait_weights(owner, p):
        pltpu.make_async_remote_copy(
            piece_of(owner, p), piece_of(owner, p), send_w.at[0], recv_w.at[owner, p], device_id=along("core", 1), device_id_type=MESH
        ).wait_recv()

    def normalize_rows(owner):
        @pl.loop(0, part // 16)
        def _(n):
            at = pl.ds(pl.multiple_of(owner * part + n * 16, 16), 16)
            features = rows_all[at, :].astype(jnp.float32)
            mean_square = jnp.mean(features * features, axis=-1, keepdims=True)
            normed[at, :] = (features * lax.rsqrt(mean_square + eps) * gain[...]).astype(jnp.bfloat16)

    keep = [
        pltpu.make_async_copy(tokens, rows_all.at[pl.ds(pl.multiple_of(lane * part, part), part)], own_sem.at[0]),
        pltpu.make_async_copy(weights, held.at[:, pl.ds(pl.multiple_of(ctx * depth, depth), depth)], own_sem.at[1]),
    ]
    for copy in keep:
        copy.start()
    pl.semaphore_wait(barrier, len(peers))

    routes = (("x", "y", 0), ("y", "x", 2))

    def owner_at(axis, by, other=0):
        if axis == "x":
            return shift(x, by) * side + shift(y, other)
        return shift(x, other) * side + shift(y, by)

    right, left, sibling = along("z", 1), along("z", -1), along("core", 1)
    lane_at = lambda by, flip=0: shift(z, by) * 2 + (1 - core if flip else core)
    send_tokens(lane, 0, right, own=True)
    send_tokens(lane, 1, left, own=True)
    for first, second, p in routes:
        send_weights(ctx, p, along(first, 1), own=True)
        send_weights(ctx, p + 1, along(first, -1), own=True)
        send_weights(ctx, p + 1, along(first, 1), own=True)
        send_weights(ctx, p, along(first, -1), own=True)
    send_tokens(lane, 1, right, own=True)
    send_tokens(lane, 0, left, own=True)
    for h in range(2):
        send_tokens(lane, h, sibling, own=True)
    for first, second, p in routes:
        send_weights(ctx, p, along(second, 1), own=True)
        send_weights(ctx, p + 1, along(second, -1), own=True)
        send_weights(ctx, p + 1, along(second, 1), own=True)
        send_weights(ctx, p, along(second, -1), own=True)
    for copy in keep:
        copy.wait()
    normalize_rows(lane)

    def spread(owner, p, axis):
        send_weights(owner, p, along(axis, 1))
        send_weights(owner, p, along(axis, -1))

    for first, second, p in routes:
        wait_weights(owner_at(first, -1), p)
        send_weights(owner_at(first, -1), p, along(first, 1))
        wait_weights(owner_at(first, 1), p + 1)
        send_weights(owner_at(first, 1), p + 1, along(first, -1))
    for first, second, p in routes:
        spread(owner_at(first, -1), p, second)
        spread(owner_at(first, 1), p + 1, second)
    for first, second, p in routes:
        wait_weights(owner_at(first, -1), p + 1)
        spread(owner_at(first, -1), p + 1, second)
        wait_weights(owner_at(first, 1), p)
        spread(owner_at(first, 1), p, second)

    def relay(by):
        for first, second, p in routes:
            owner = owner_at(first, by, -1)
            wait_weights(owner, p)
            send_weights(owner, p, along(second, 1))
            owner = owner_at(first, by, 1)
            wait_weights(owner, p + 1)
            send_weights(owner, p + 1, along(second, -1))

    for first, second, p in routes:
        for q in (p, p + 1):
            wait_weights(owner_at(first, 2), q)
            spread(owner_at(first, 2), q, second)
    relay(0)
    wait_tokens(lane_at(-1), 0)
    send_tokens(lane_at(-1), 0, right)
    send_tokens(lane_at(-1), 0, sibling)
    wait_tokens(lane_at(1), 1)
    send_tokens(lane_at(1), 1, left)
    send_tokens(lane_at(1), 1, sibling)
    relay(-1)
    relay(1)
    for h in range(2):
        wait_tokens(lane_at(0, 1), h)
    normalize_rows(lane_at(0, 1))
    wait_tokens(lane_at(-1), 1)
    send_tokens(lane_at(-1), 1, sibling)
    wait_tokens(lane_at(1), 0)
    send_tokens(lane_at(1), 0, sibling)
    normalize_rows(lane_at(-1))
    normalize_rows(lane_at(1))
    relay(2)
    for by in (-1, 1):
        for h in range(2):
            wait_tokens(lane_at(by, 1), h)
        normalize_rows(lane_at(by, 1))
    for h in range(2):
        wait_tokens(lane_at(2), h)
        send_tokens(lane_at(2), h, sibling)
    normalize_rows(lane_at(2))
    for first, second, p in routes:
        for by in (0, -1, 1, 2):
            wait_weights(owner_at(first, by, -1), p + 1)
            wait_weights(owner_at(first, by, 1), p)
            wait_weights(owner_at(first, by, 2), p)
            wait_weights(owner_at(first, by, 2), p + 1)
    for h in range(2):
        wait_tokens(lane_at(2, 1), h)
    normalize_rows(lane_at(2, 1))

    tile = 256
    steps = normed.shape[0] // tile
    give = pltpu.make_async_copy(held.at[3], projection, own_sem.at[0])
    give.start()

    @pl.loop(0, 3 * steps)
    def _(n):
        which, at = n // steps, pl.ds(pl.multiple_of(lax.rem(n, steps) * tile, tile), tile)
        projected[which, at, :] = jnp.dot(normed[at, :], held[which], preferred_element_type=jnp.float32).astype(jnp.bfloat16)

    give.wait()
    for _, copy in sent:
        copy.wait_send()


def gather_and_project(tokens, norm_gain, qkv_weight, out_weight, side, lanes):
    part, width = tokens.shape
    columns = qkv_weight.shape[2]
    weights = jnp.concatenate([qkv_weight, out_weight[None]], axis=0)
    vmem = pl.BlockSpec(memory_space=pltpu.VMEM)
    return pl.pallas_call(
        functools.partial(gather_kernel, side, EPSILON),
        out_shape=[
            jax.ShapeDtypeStruct((3, lanes * part, columns), jnp.bfloat16),
            jax.ShapeDtypeStruct((width, columns), jnp.bfloat16),
        ],
        in_specs=[vmem] * 3,
        out_specs=[vmem] * 2,
        scratch_shapes=[
            pltpu.VMEM((lanes * part, width), jnp.bfloat16),
            pltpu.VMEM((lanes * part, width), jnp.bfloat16),
            pltpu.VMEM((4, width, columns), jnp.bfloat16),
            pltpu.SemaphoreType.DMA((14,)),
            pltpu.SemaphoreType.DMA((lanes, 2)),
            pltpu.SemaphoreType.DMA((60,)),
            pltpu.SemaphoreType.DMA((side * side, 4)),
            pltpu.SemaphoreType.DMA((2,)),
        ],
        compiler_params=pltpu.CompilerParams(
            collective_id=1, has_side_effects=True, vmem_limit_bytes=60 * 2**20
        ),
    )(tokens, norm_gain[None, :], weights)


def shards(spans, lanes, tokens, norm_gain, qkv_weight, out_weight, layout):
    side = math.isqrt(spans)
    projected, projection = gather_and_project(tokens, norm_gain, qkv_weight, out_weight, side, lanes)
    projection = projection.reshape(spans, -1, projection.shape[1])
    return attend_and_reduce(projected[0], projected[1], projected[2], projection, layout, spans)


def solution(mesh):
    placed = (P(("ctx", "fsdp"), None), P(), P(None, "ctx", "fsdp"), P("fsdp", "ctx"), P())
    return jax.shard_map(
        functools.partial(shards, mesh.shape["ctx"], mesh.shape["fsdp"]),
        mesh=mesh, in_specs=placed, out_specs=P(("ctx", "fsdp"), None), check_vma=False,
    )
```

```python
import functools
import math

import jax
import jax.numpy as jnp
from jax import lax
from jax.experimental import pallas as pl
from jax.experimental.pallas import tpu as pltpu
from jax.sharding import PartitionSpec as P

HEAD_DIM = 128
BLK = 128
EPSILON = 1e-05
CAP = 2
MESH = pl.DeviceIdType.MESH


def block_tables(layout, spans):
    me = lax.axis_index("ctx")
    blocks, listed = layout.shape
    own = blocks // spans
    entries = layout.reshape(spans, own * listed)
    home, within = entries // own, entries % own
    mine = home == me
    lowest = jnp.min(jnp.where(mine, within, own - 1), axis=1)
    highest = jnp.max(jnp.where(mine, within, 0), axis=1)
    pick = jnp.stack([lowest, highest], axis=1).reshape(-1)
    rows = lax.dynamic_index_in_dim(entries, me, 0, keepdims=False)
    row_home, row_within = rows // own, rows % own
    same = row_home[:, None] == row_home[None, :]
    low = jnp.min(jnp.where(same, row_within[None, :], own - 1), axis=1)
    far = own + CAP * row_home + jnp.where(row_within == low, 0, 1)
    listed_slot = jnp.where(row_home == me, row_within, far).reshape(own, listed)
    index = jnp.arange(own, dtype=jnp.int32)
    block = me * own + index
    before = jnp.where(index > 0, index - 1, jnp.where(me > 0, own + CAP * spans, 0))
    slot = jnp.concatenate([index[:, None], before[:, None], listed_slot], axis=1)
    gap = block[:, None] - rows.reshape(own, listed)
    before_gap = jnp.where(block > 0, 1, -1)
    reach = jnp.concatenate([jnp.zeros_like(index)[:, None], before_gap[:, None], gap], axis=1) * BLK
    return pick.astype(jnp.int32), slot.reshape(-1).astype(jnp.int32), reach.reshape(-1).astype(jnp.int32)


def attend_kernel(
    spans, slots, pick, slot, reach, projected, projection, out,
    kpool, vpool, kstage, vstage, scores, attended, partial, crossed, packed, hop, final,
    own_sem, send_sem, recv_sem, cross_sem, sum_send, sum_recv,
):
    me, lane = lax.axis_index("ctx"), lax.axis_index("fsdp")
    q, k, v = (projected.at[which] for which in range(3))
    z, core = lane // 2, lax.rem(lane, 2)
    chips = 4
    pieces = projection.shape[0]
    wide = projection.shape[2]
    half = pieces // 2
    right = (me, lax.rem(z + 1, chips) * 2 + core)
    left = (me, lax.rem(z + chips - 1, chips) * 2 + core)
    sibling = (me, z * 2 + 1 - core)
    own = q.shape[0]
    heads = q.shape[2] // HEAD_DIM
    barrier = pltpu.get_barrier_semaphore()

    @pl.loop(1, spans)
    def _(step):
        peer = lax.rem(me + step, spans)
        pl.semaphore_signal(barrier, inc=1, device_id=(peer, lane), device_id_type=MESH)

    for peer in (right, left, sibling):
        pl.semaphore_signal(barrier, inc=1, device_id=peer, device_id_type=MESH)

    keep = [
        pltpu.make_async_copy(k, kpool.at[pl.ds(0, own)], own_sem.at[0]),
        pltpu.make_async_copy(v, vpool.at[pl.ds(0, own)], own_sem.at[1]),
    ]
    for copy in keep:
        copy.start()

    @pl.loop(0, spans * CAP)
    def _(n):
        kstage[n] = k[pick[n]]
        vstage[n] = v[pick[n]]

    pl.semaphore_wait(barrier, spans + 2)

    def listed(src, dst):
        there = pl.ds(own + CAP * src, CAP)
        return [
            pltpu.make_async_remote_copy(
                stage.at[pl.ds(CAP * dst, CAP)], pool.at[there],
                send_sem.at[dst, j], recv_sem.at[src, j], device_id=(dst, lane), device_id_type=MESH,
            )
            for j, (stage, pool) in enumerate(((kstage, kpool), (vstage, vpool)))
        ]

    def previous(dst):
        there = own + CAP * spans
        return [
            pltpu.make_async_remote_copy(
                mine.at[own - 1], pool.at[there],
                send_sem.at[spans, j], recv_sem.at[spans, j], device_id=(dst, lane), device_id_type=MESH,
            )
            for j, (mine, pool) in enumerate(((k, kpool), (v, vpool)))
        ]

    @pl.when(me < spans - 1)
    def _():
        for copy in previous(me + 1):
            copy.start()

    @pl.loop(1, spans)
    def _(step):
        @pl.when(me + step < spans)
        def _():
            for copy in listed(me, me + step):
                copy.start()

    for copy in keep:
        copy.wait()

    @pl.when(me > 0)
    def _():
        for copy in previous(me):
            copy.wait_recv()

    @pl.loop(1, spans)
    def _(step):
        @pl.when(me >= step)
        def _():
            for copy in listed(me - step, me):
                copy.wait_recv()

    offset = lax.broadcasted_iota(jnp.int32, (BLK, BLK), 1) - lax.broadcasted_iota(jnp.int32, (BLK, BLK), 0)

    def attend(b, at):
        for head in range(heads):
            columns = pl.ds(head * HEAD_DIM, HEAD_DIM)
            query = q[b, :, columns]
            top = jnp.full((BLK, BLK), -1e30, jnp.float32)
            for n in range(slots):
                keys = kpool[slot[b * slots + n], :, columns]
                part = lax.dot_general(query, keys, (((1,), (1,)), ((), ())), preferred_element_type=jnp.float32)
                part = jnp.where(offset <= reach[b * slots + n], part * HEAD_DIM**-0.5, -1e30)
                scores[n] = part
                top = jnp.maximum(top, part)
            top = jnp.max(top, axis=1, keepdims=True)
            total = jnp.zeros((BLK, BLK), jnp.float32)
            blended = jnp.zeros((BLK, HEAD_DIM), jnp.float32)
            for n in range(slots):
                weights = jnp.exp(scores[n] - top)
                total += weights
                values = vpool[slot[b * slots + n], :, columns]
                blended += jnp.dot(weights.astype(jnp.bfloat16), values, preferred_element_type=jnp.float32)
            total = jnp.sum(total, axis=1, keepdims=True)
            attended[at, :, columns] = (blended / total).astype(jnp.bfloat16)

    def cross(g):
        return pltpu.make_async_remote_copy(
            partial.at[g, 0], crossed.at[g], cross_sem.at[0, g], cross_sem.at[1, g], device_id=sibling, device_id_type=MESH
        )

    def travel(n, source, target, peer):
        return pltpu.make_async_remote_copy(
            source, target, sum_send.at[n], sum_recv.at[n], device_id=peer, device_id_type=MESH
        )

    first, second = pl.ds(0, half), pl.ds(half, half)
    travels = [
        travel(0, packed.at[0, first], hop.at[0], right),
        travel(1, packed.at[0, second], hop.at[1], left),
        travel(2, packed.at[1, second], final.at[0, second], right),
        travel(3, packed.at[1, first], final.at[0, first], right),
        travel(4, packed.at[2, first], final.at[1, first], left),
        travel(5, packed.at[2, second], final.at[1, second], left),
    ]

    def add(g, low, more=None):
        @pl.loop(0, half)
        def _(n):
            term = partial[g, 1, low + n].astype(jnp.float32) + crossed[g, low + n].astype(jnp.float32)
            if more is not None:
                term += hop[more, n].astype(jnp.float32)
            packed[g, low + n] = term.astype(jnp.bfloat16)

    for g, steps in enumerate((2, 1, -1, 0)):
        chip = lax.rem(z + steps + chips, chips)

        @pl.loop(0, 2)
        def _(turn):
            attend(chip * 2 + lax.rem(core + 1 + turn, 2), turn)

            @pl.loop(0, pieces)
            def _(n):
                partial[g, turn, n] = jnp.dot(
                    attended[turn], projection[n], preferred_element_type=jnp.float32
                ).astype(jnp.bfloat16)

            @pl.when(turn == 0)
            def _():
                cross(g).start()

        cross(g).wait_recv()
        if g == 0:
            add(0, 0)
            travels[0].start()
            add(0, half)
            travels[1].start()
        elif g == 1:
            add(1, half)
            travels[2].start()
        elif g == 2:
            add(2, 0)
            travels[4].start()
            travels[0].wait_recv()
            add(1, 0, 0)
            travels[3].start()
            travels[1].wait_recv()
            add(2, half, 1)
            travels[5].start()

    for low, waits in ((half, (2, 5)), (0, (3, 4))):
        for n in waits:
            travels[n].wait_recv()

        @pl.loop(0, half)
        def _(n):
            at = low + n
            term = partial[3, 1, at].astype(jnp.float32) + crossed[3, at].astype(jnp.float32)
            term += final[0, at].astype(jnp.float32) + final[1, at].astype(jnp.float32)
            out[:, pl.ds(pl.multiple_of(at * wide, wide), wide)] = term.astype(jnp.bfloat16)

    for g in range(chips):
        cross(g).wait_send()
    for copy in travels:
        copy.wait_send()

    @pl.when(me < spans - 1)
    def _():
        for copy in previous(me + 1):
            copy.wait_send()

    @pl.loop(1, spans)
    def _(step):
        @pl.when(me + step < spans)
        def _():
            for copy in listed(me, me + step):
                copy.wait_send()


def attend_and_reduce(projected, projection, layout, spans):
    _, rows, width = projected.shape
    slots = 2 + layout.shape[1]
    pick, slot, reach = block_tables(layout, spans)
    own = rows // BLK
    pool = own + CAP * spans + 1
    pieces, _, wide = projection.shape
    whole = (pieces, BLK, wide)
    projected = projected.reshape(3, own, BLK, width)
    smem = pl.BlockSpec(memory_space=pltpu.SMEM)
    vmem = pl.BlockSpec(memory_space=pltpu.VMEM)
    return pl.pallas_call(
        functools.partial(attend_kernel, spans, slots),
        out_shape=jax.ShapeDtypeStruct((BLK, pieces * wide), jnp.bfloat16),
        in_specs=[smem] * 3 + [vmem] * 2,
        out_specs=vmem,
        scratch_shapes=[
            pltpu.VMEM((pool, BLK, width), jnp.bfloat16),
            pltpu.VMEM((pool, BLK, width), jnp.bfloat16),
            pltpu.VMEM((spans * CAP, BLK, width), jnp.bfloat16),
            pltpu.VMEM((spans * CAP, BLK, width), jnp.bfloat16),
            pltpu.VMEM((slots, BLK, BLK), jnp.float32),
            pltpu.VMEM((2, BLK, width), jnp.bfloat16),
            pltpu.VMEM((4, 2, *whole), jnp.bfloat16),
            pltpu.VMEM((4, *whole), jnp.bfloat16),
            pltpu.VMEM((3, *whole), jnp.bfloat16),
            pltpu.VMEM((2, pieces // 2, BLK, wide), jnp.bfloat16),
            pltpu.VMEM((2, *whole), jnp.bfloat16),
            pltpu.SemaphoreType.DMA((2,)),
            pltpu.SemaphoreType.DMA((spans + 1, 2)),
            pltpu.SemaphoreType.DMA((spans + 1, 2)),
            pltpu.SemaphoreType.DMA((2, 4)),
            pltpu.SemaphoreType.DMA((6,)),
            pltpu.SemaphoreType.DMA((6,)),
        ],
        compiler_params=pltpu.CompilerParams(
            collective_id=0, has_side_effects=True, vmem_limit_bytes=60 * 2**20
        ),
    )(pick, slot, reach, projected, projection)


def gather_kernel(side, eps, tokens, gain, weights, projected, projection, rows_all, normed, held, send_t, recv_t, send_w, recv_w, own_sem):
    ctx, lane = lax.axis_index("ctx"), lax.axis_index("fsdp")
    x, y = ctx // side, lax.rem(ctx, side)
    z, core = lane // 2, lax.rem(lane, 2)
    part, width = tokens.shape
    depth = weights.shape[1]
    half, quarter = part // 2, depth // 4

    def shift(at, by):
        return lax.rem(at + by + side, side)

    def along(axis, by):
        if axis == "x":
            return (shift(x, by) * side + y, lane)
        if axis == "y":
            return (x * side + shift(y, by), lane)
        if axis == "z":
            return (ctx, shift(z, by) * 2 + core)
        return (ctx, z * 2 + 1 - core)

    barrier = pltpu.get_barrier_semaphore()
    peers = [along(axis, by) for axis in "xyz" for by in (1, -1)] + [along("core", 1)]
    for peer in peers:
        pl.semaphore_signal(barrier, inc=1, device_id=peer, device_id_type=MESH)

    sent = []

    def send_tokens(owner, h, peer, own=False):
        there = rows_all.at[pl.ds(pl.multiple_of(owner * part + h * half, half), half)]
        here = tokens.at[pl.ds(h * half, half)] if own else there
        copy = pltpu.make_async_remote_copy(
            here, there, send_t.at[len([c for c in sent if c[0] == "t"])], recv_t.at[owner, h], device_id=peer, device_id_type=MESH
        )
        copy.start()
        sent.append(("t", copy))

    def wait_tokens(owner, h):
        there = rows_all.at[pl.ds(pl.multiple_of(owner * part + h * half, half), half)]
        pltpu.make_async_remote_copy(
            there, there, send_t.at[0], recv_t.at[owner, h], device_id=along("core", 1), device_id_type=MESH
        ).wait_recv()

    def piece_of(owner, p):
        return held.at[:, pl.ds(pl.multiple_of(owner * depth + p * quarter, quarter), quarter)]

    def send_weights(owner, p, peer, own=False):
        there = piece_of(owner, p)
        here = weights.at[:, pl.ds(p * quarter, quarter)] if own else there
        copy = pltpu.make_async_remote_copy(
            here, there, send_w.at[len([c for c in sent if c[0] == "w"])], recv_w.at[owner, p], device_id=peer, device_id_type=MESH
        )
        copy.start()
        sent.append(("w", copy))

    def wait_weights(owner, p):
        pltpu.make_async_remote_copy(
            piece_of(owner, p), piece_of(owner, p), send_w.at[0], recv_w.at[owner, p], device_id=along("core", 1), device_id_type=MESH
        ).wait_recv()

    def normalize_rows(owner):
        @pl.loop(0, part // 16)
        def _(n):
            at = pl.ds(pl.multiple_of(owner * part + n * 16, 16), 16)
            features = rows_all[at, :].astype(jnp.float32)
            mean_square = jnp.mean(features * features, axis=-1, keepdims=True)
            normed[at, :] = (features * lax.rsqrt(mean_square + eps) * gain[...]).astype(jnp.bfloat16)

    keep = [
        pltpu.make_async_copy(tokens, rows_all.at[pl.ds(pl.multiple_of(lane * part, part), part)], own_sem.at[0]),
        pltpu.make_async_copy(weights, held.at[:, pl.ds(pl.multiple_of(ctx * depth, depth), depth)], own_sem.at[1]),
    ]
    for copy in keep:
        copy.start()
    pl.semaphore_wait(barrier, len(peers))

    routes = (("x", "y", 0), ("y", "x", 2))

    def owner_at(axis, by, other=0):
        if axis == "x":
            return shift(x, by) * side + shift(y, other)
        return shift(x, other) * side + shift(y, by)

    right, left, sibling = along("z", 1), along("z", -1), along("core", 1)
    lane_at = lambda by, flip=0: shift(z, by) * 2 + (1 - core if flip else core)
    send_tokens(lane, 0, right, own=True)
    send_tokens(lane, 1, left, own=True)
    for first, second, p in routes:
        send_weights(ctx, p, along(first, 1), own=True)
        send_weights(ctx, p + 1, along(first, -1), own=True)
        send_weights(ctx, p + 1, along(first, 1), own=True)
        send_weights(ctx, p, along(first, -1), own=True)
    send_tokens(lane, 1, right, own=True)
    send_tokens(lane, 0, left, own=True)
    for h in range(2):
        send_tokens(lane, h, sibling, own=True)
    for first, second, p in routes:
        send_weights(ctx, p, along(second, 1), own=True)
        send_weights(ctx, p + 1, along(second, -1), own=True)
        send_weights(ctx, p + 1, along(second, 1), own=True)
        send_weights(ctx, p, along(second, -1), own=True)
    for copy in keep:
        copy.wait()
    normalize_rows(lane)

    def spread(owner, p, axis):
        send_weights(owner, p, along(axis, 1))
        send_weights(owner, p, along(axis, -1))

    for first, second, p in routes:
        wait_weights(owner_at(first, -1), p)
        send_weights(owner_at(first, -1), p, along(first, 1))
        wait_weights(owner_at(first, 1), p + 1)
        send_weights(owner_at(first, 1), p + 1, along(first, -1))
    for first, second, p in routes:
        spread(owner_at(first, -1), p, second)
        spread(owner_at(first, 1), p + 1, second)
    for first, second, p in routes:
        wait_weights(owner_at(first, -1), p + 1)
        spread(owner_at(first, -1), p + 1, second)
        wait_weights(owner_at(first, 1), p)
        spread(owner_at(first, 1), p, second)

    def relay(by):
        for first, second, p in routes:
            owner = owner_at(first, by, -1)
            wait_weights(owner, p)
            send_weights(owner, p, along(second, 1))
            owner = owner_at(first, by, 1)
            wait_weights(owner, p + 1)
            send_weights(owner, p + 1, along(second, -1))

    for first, second, p in routes:
        for q in (p, p + 1):
            wait_weights(owner_at(first, 2), q)
            spread(owner_at(first, 2), q, second)
    relay(0)
    wait_tokens(lane_at(-1), 0)
    send_tokens(lane_at(-1), 0, right)
    send_tokens(lane_at(-1), 0, sibling)
    wait_tokens(lane_at(1), 1)
    send_tokens(lane_at(1), 1, left)
    send_tokens(lane_at(1), 1, sibling)
    relay(-1)
    relay(1)
    for h in range(2):
        wait_tokens(lane_at(0, 1), h)
    normalize_rows(lane_at(0, 1))
    wait_tokens(lane_at(-1), 1)
    send_tokens(lane_at(-1), 1, sibling)
    wait_tokens(lane_at(1), 0)
    send_tokens(lane_at(1), 0, sibling)
    normalize_rows(lane_at(-1))
    normalize_rows(lane_at(1))
    relay(2)
    for by in (-1, 1):
        for h in range(2):
            wait_tokens(lane_at(by, 1), h)
        normalize_rows(lane_at(by, 1))
    for h in range(2):
        wait_tokens(lane_at(2), h)
        send_tokens(lane_at(2), h, sibling)
    normalize_rows(lane_at(2))
    for first, second, p in routes:
        for by in (0, -1, 1, 2):
            wait_weights(owner_at(first, by, -1), p + 1)
            wait_weights(owner_at(first, by, 1), p)
            wait_weights(owner_at(first, by, 2), p)
            wait_weights(owner_at(first, by, 2), p + 1)
    for h in range(2):
        wait_tokens(lane_at(2, 1), h)
    normalize_rows(lane_at(2, 1))

    tile = 256
    steps = normed.shape[0] // tile
    give = pltpu.make_async_copy(held.at[3], projection, own_sem.at[0])
    give.start()

    @pl.loop(0, 3 * steps)
    def _(n):
        which, at = n // steps, pl.ds(pl.multiple_of(lax.rem(n, steps) * tile, tile), tile)
        projected[which, at, :] = jnp.dot(normed[at, :], held[which], preferred_element_type=jnp.float32).astype(jnp.bfloat16)

    give.wait()
    for _, copy in sent:
        copy.wait_send()


def gather_and_project(tokens, norm_gain, qkv_weight, out_weight, side, lanes):
    part, width = tokens.shape
    columns = qkv_weight.shape[2]
    weights = jnp.concatenate([qkv_weight, out_weight[None]], axis=0)
    vmem = pl.BlockSpec(memory_space=pltpu.VMEM)
    return pl.pallas_call(
        functools.partial(gather_kernel, side, EPSILON),
        out_shape=[
            jax.ShapeDtypeStruct((3, lanes * part, columns), jnp.bfloat16),
            jax.ShapeDtypeStruct((width, columns), jnp.bfloat16),
        ],
        in_specs=[vmem] * 3,
        out_specs=[vmem] * 2,
        scratch_shapes=[
            pltpu.VMEM((lanes * part, width), jnp.bfloat16),
            pltpu.VMEM((lanes * part, width), jnp.bfloat16),
            pltpu.VMEM((4, width, columns), jnp.bfloat16),
            pltpu.SemaphoreType.DMA((14,)),
            pltpu.SemaphoreType.DMA((lanes, 2)),
            pltpu.SemaphoreType.DMA((60,)),
            pltpu.SemaphoreType.DMA((side * side, 4)),
            pltpu.SemaphoreType.DMA((2,)),
        ],
        compiler_params=pltpu.CompilerParams(
            collective_id=1, has_side_effects=True, vmem_limit_bytes=60 * 2**20
        ),
    )(tokens, norm_gain[None, :], weights)


def shards(spans, lanes, tokens, norm_gain, qkv_weight, out_weight, layout):
    side = math.isqrt(spans)
    projected, projection = gather_and_project(tokens, norm_gain, qkv_weight, out_weight, side, lanes)
    projection = projection.reshape(spans, -1, projection.shape[1])
    return attend_and_reduce(projected, projection, layout, spans)


def solution(mesh):
    placed = (P(("ctx", "fsdp"), None), P(), P(None, "ctx", "fsdp"), P("fsdp", "ctx"), P())
    return jax.shard_map(
        functools.partial(shards, mesh.shape["ctx"], mesh.shape["fsdp"]),
        mesh=mesh, in_specs=placed, out_specs=P(("ctx", "fsdp"), None), check_vma=False,
    )
```

```python
import functools
import math

import jax
import jax.numpy as jnp
from jax import lax
from jax.experimental import pallas as pl
from jax.experimental.pallas import tpu as pltpu
from jax.sharding import PartitionSpec as P

HEAD_DIM = 128
BLK = 128
EPSILON = 1e-05
CAP = 2
MESH = pl.DeviceIdType.MESH


def block_tables(layout, spans):
    me = lax.axis_index("ctx")
    blocks, listed = layout.shape
    own = blocks // spans
    entries = layout.reshape(spans, own * listed)
    home, within = entries // own, entries % own
    mine = home == me
    lowest = jnp.min(jnp.where(mine, within, own - 1), axis=1)
    highest = jnp.max(jnp.where(mine, within, 0), axis=1)
    pick = jnp.stack([lowest, highest], axis=1).reshape(-1)
    rows = lax.dynamic_index_in_dim(entries, me, 0, keepdims=False)
    row_home, row_within = rows // own, rows % own
    same = row_home[:, None] == row_home[None, :]
    low = jnp.min(jnp.where(same, row_within[None, :], own - 1), axis=1)
    far = own + CAP * row_home + jnp.where(row_within == low, 0, 1)
    listed_slot = jnp.where(row_home == me, row_within, far).reshape(own, listed)
    index = jnp.arange(own, dtype=jnp.int32)
    block = me * own + index
    before = jnp.where(index > 0, index - 1, jnp.where(me > 0, own + CAP * spans, 0))
    slot = jnp.concatenate([index[:, None], before[:, None], listed_slot], axis=1)
    gap = block[:, None] - rows.reshape(own, listed)
    before_gap = jnp.where(block > 0, 1, -1)
    reach = jnp.concatenate([jnp.zeros_like(index)[:, None], before_gap[:, None], gap], axis=1) * BLK
    return pick.astype(jnp.int32), slot.reshape(-1).astype(jnp.int32), reach.reshape(-1).astype(jnp.int32)


def gather(side, eps, enter, tokens, gain, weights, rows_all, normed, held, send_t, recv_t, send_w, recv_w, own_sem):
    ctx, lane = lax.axis_index("ctx"), lax.axis_index("fsdp")
    x, y = ctx // side, lax.rem(ctx, side)
    z, core = lane // 2, lax.rem(lane, 2)
    part, width = tokens.shape
    depth = weights.shape[1]
    half, quarter = part // 2, depth // 4

    def shift(at, by):
        return lax.rem(at + by + side, side)

    def along(axis, by):
        if axis == "x":
            return (shift(x, by) * side + y, lane)
        if axis == "y":
            return (x * side + shift(y, by), lane)
        if axis == "z":
            return (ctx, shift(z, by) * 2 + core)
        return (ctx, z * 2 + 1 - core)

    sent = []

    def send_tokens(owner, h, peer, own=False):
        there = rows_all.at[pl.ds(pl.multiple_of(owner * part + h * half, half), half)]
        here = tokens.at[pl.ds(h * half, half)] if own else there
        copy = pltpu.make_async_remote_copy(
            here, there, send_t.at[len([c for c in sent if c[0] == "t"])], recv_t.at[owner, h], device_id=peer, device_id_type=MESH
        )
        copy.start()
        sent.append(("t", copy))

    def wait_tokens(owner, h):
        there = rows_all.at[pl.ds(pl.multiple_of(owner * part + h * half, half), half)]
        pltpu.make_async_remote_copy(
            there, there, send_t.at[0], recv_t.at[owner, h], device_id=along("core", 1), device_id_type=MESH
        ).wait_recv()

    def piece_of(owner, p):
        return held.at[:, pl.ds(pl.multiple_of(owner * depth + p * quarter, quarter), quarter)]

    def send_weights(owner, p, peer, own=False):
        there = piece_of(owner, p)
        here = weights.at[:, pl.ds(p * quarter, quarter)] if own else there
        copy = pltpu.make_async_remote_copy(
            here, there, send_w.at[len([c for c in sent if c[0] == "w"])], recv_w.at[owner, p], device_id=peer, device_id_type=MESH
        )
        copy.start()
        sent.append(("w", copy))

    def wait_weights(owner, p):
        pltpu.make_async_remote_copy(
            piece_of(owner, p), piece_of(owner, p), send_w.at[0], recv_w.at[owner, p], device_id=along("core", 1), device_id_type=MESH
        ).wait_recv()

    def normalize_rows(owner):
        @pl.loop(0, part // 16)
        def _(n):
            at = pl.ds(pl.multiple_of(owner * part + n * 16, 16), 16)
            features = rows_all[at, :].astype(jnp.float32)
            mean_square = jnp.mean(features * features, axis=-1, keepdims=True)
            normed[at, :] = (features * lax.rsqrt(mean_square + eps) * gain[...]).astype(jnp.bfloat16)

    keep = [
        pltpu.make_async_copy(tokens, rows_all.at[pl.ds(pl.multiple_of(lane * part, part), part)], own_sem.at[0]),
        pltpu.make_async_copy(weights, held.at[:, pl.ds(pl.multiple_of(ctx * depth, depth), depth)], own_sem.at[1]),
    ]
    for copy in keep:
        copy.start()
    enter()

    routes = (("x", "y", 0), ("y", "x", 2))

    def owner_at(axis, by, other=0):
        if axis == "x":
            return shift(x, by) * side + shift(y, other)
        return shift(x, other) * side + shift(y, by)

    right, left, sibling = along("z", 1), along("z", -1), along("core", 1)
    lane_at = lambda by, flip=0: shift(z, by) * 2 + (1 - core if flip else core)
    send_tokens(lane, 0, right, own=True)
    send_tokens(lane, 1, left, own=True)
    for first, second, p in routes:
        send_weights(ctx, p, along(first, 1), own=True)
        send_weights(ctx, p + 1, along(first, -1), own=True)
        send_weights(ctx, p + 1, along(first, 1), own=True)
        send_weights(ctx, p, along(first, -1), own=True)
    send_tokens(lane, 1, right, own=True)
    send_tokens(lane, 0, left, own=True)
    for h in range(2):
        send_tokens(lane, h, sibling, own=True)
    for first, second, p in routes:
        send_weights(ctx, p, along(second, 1), own=True)
        send_weights(ctx, p + 1, along(second, -1), own=True)
        send_weights(ctx, p + 1, along(second, 1), own=True)
        send_weights(ctx, p, along(second, -1), own=True)
    for copy in keep:
        copy.wait()
    normalize_rows(lane)

    def spread(owner, p, axis):
        send_weights(owner, p, along(axis, 1))
        send_weights(owner, p, along(axis, -1))

    for first, second, p in routes:
        wait_weights(owner_at(first, -1), p)
        send_weights(owner_at(first, -1), p, along(first, 1))
        wait_weights(owner_at(first, 1), p + 1)
        send_weights(owner_at(first, 1), p + 1, along(first, -1))
    for first, second, p in routes:
        spread(owner_at(first, -1), p, second)
        spread(owner_at(first, 1), p + 1, second)
    for first, second, p in routes:
        wait_weights(owner_at(first, -1), p + 1)
        spread(owner_at(first, -1), p + 1, second)
        wait_weights(owner_at(first, 1), p)
        spread(owner_at(first, 1), p, second)

    def relay(by):
        for first, second, p in routes:
            owner = owner_at(first, by, -1)
            wait_weights(owner, p)
            send_weights(owner, p, along(second, 1))
            owner = owner_at(first, by, 1)
            wait_weights(owner, p + 1)
            send_weights(owner, p + 1, along(second, -1))

    for first, second, p in routes:
        for q in (p, p + 1):
            wait_weights(owner_at(first, 2), q)
            spread(owner_at(first, 2), q, second)
    relay(0)
    wait_tokens(lane_at(-1), 0)
    send_tokens(lane_at(-1), 0, right)
    send_tokens(lane_at(-1), 0, sibling)
    wait_tokens(lane_at(1), 1)
    send_tokens(lane_at(1), 1, left)
    send_tokens(lane_at(1), 1, sibling)
    relay(-1)
    relay(1)
    for h in range(2):
        wait_tokens(lane_at(0, 1), h)
    normalize_rows(lane_at(0, 1))
    wait_tokens(lane_at(-1), 1)
    send_tokens(lane_at(-1), 1, sibling)
    wait_tokens(lane_at(1), 0)
    send_tokens(lane_at(1), 0, sibling)
    normalize_rows(lane_at(-1))
    normalize_rows(lane_at(1))
    relay(2)
    for by in (-1, 1):
        for h in range(2):
            wait_tokens(lane_at(by, 1), h)
        normalize_rows(lane_at(by, 1))
    for h in range(2):
        wait_tokens(lane_at(2), h)
        send_tokens(lane_at(2), h, sibling)
    normalize_rows(lane_at(2))
    for first, second, p in routes:
        for by in (0, -1, 1, 2):
            wait_weights(owner_at(first, by, -1), p + 1)
            wait_weights(owner_at(first, by, 1), p)
            wait_weights(owner_at(first, by, 2), p)
            wait_weights(owner_at(first, by, 2), p + 1)
    for h in range(2):
        wait_tokens(lane_at(2, 1), h)
    normalize_rows(lane_at(2, 1))

    return [copy for _, copy in sent]


def attend_kernel(
    side, spans, slots, pick, slot, reach, tokens, gain, weights, out, rows_all, normed, held, projected,
    kpool, vpool, kstage, vstage, scores, attended, partial, crossed, packed, hop, final,
    send_t, recv_t, send_w, recv_w, own_sem, send_sem, recv_sem, cross_sem, sum_send, sum_recv,
):
    me, lane = lax.axis_index("ctx"), lax.axis_index("fsdp")
    q, k, v = (projected.at[which] for which in range(3))
    z, core = lane // 2, lax.rem(lane, 2)
    chips = 4
    pieces, wide = spans, held.shape[2]
    projection = held.at[3]
    half = pieces // 2
    right = (me, lax.rem(z + 1, chips) * 2 + core)
    left = (me, lax.rem(z + chips - 1, chips) * 2 + core)
    sibling = (me, z * 2 + 1 - core)
    own = q.shape[0]
    width = q.shape[2]
    heads = width // HEAD_DIM
    barrier = pltpu.get_barrier_semaphore()

    @pl.loop(1, spans)
    def _(step):
        peer = lax.rem(me + step, spans)
        pl.semaphore_signal(barrier, inc=1, device_id=(peer, lane), device_id_type=MESH)

    for peer in (right, left, sibling):
        pl.semaphore_signal(barrier, inc=1, device_id=peer, device_id_type=MESH)

    sent = gather(
        side, EPSILON, lambda: pl.semaphore_wait(barrier, spans + 2), tokens, gain, weights,
        rows_all, normed, held, send_t, recv_t, send_w, recv_w, own_sem,
    )
    tile = 2 * BLK

    def project(which):
        @pl.loop(0, normed.shape[0] // tile)
        def _(n):
            rows = normed[pl.ds(pl.multiple_of(n * tile, tile), tile), :]
            product = jnp.dot(rows, held[which], preferred_element_type=jnp.float32)
            projected[which, pl.ds(2 * n, 2)] = product.astype(jnp.bfloat16).reshape(2, BLK, width)

    project(1)
    project(2)
    keep = [
        pltpu.make_async_copy(k, kpool.at[pl.ds(0, own)], own_sem.at[0]),
        pltpu.make_async_copy(v, vpool.at[pl.ds(0, own)], own_sem.at[1]),
    ]
    for copy in keep:
        copy.start()

    @pl.loop(0, spans * CAP)
    def _(n):
        kstage[n] = k[pick[n]]
        vstage[n] = v[pick[n]]

    def listed(src, dst):
        there = pl.ds(own + CAP * src, CAP)
        return [
            pltpu.make_async_remote_copy(
                stage.at[pl.ds(CAP * dst, CAP)], pool.at[there],
                send_sem.at[dst, j], recv_sem.at[src, j], device_id=(dst, lane), device_id_type=MESH,
            )
            for j, (stage, pool) in enumerate(((kstage, kpool), (vstage, vpool)))
        ]

    def previous(dst):
        there = own + CAP * spans
        return [
            pltpu.make_async_remote_copy(
                mine.at[own - 1], pool.at[there],
                send_sem.at[spans, j], recv_sem.at[spans, j], device_id=(dst, lane), device_id_type=MESH,
            )
            for j, (mine, pool) in enumerate(((k, kpool), (v, vpool)))
        ]

    @pl.when(me < spans - 1)
    def _():
        for copy in previous(me + 1):
            copy.start()

    @pl.loop(1, spans)
    def _(step):
        @pl.when(me + step < spans)
        def _():
            for copy in listed(me, me + step):
                copy.start()

    project(0)
    for copy in keep:
        copy.wait()

    @pl.when(me > 0)
    def _():
        for copy in previous(me):
            copy.wait_recv()

    @pl.loop(1, spans)
    def _(step):
        @pl.when(me >= step)
        def _():
            for copy in listed(me - step, me):
                copy.wait_recv()

    offset = lax.broadcasted_iota(jnp.int32, (BLK, BLK), 1) - lax.broadcasted_iota(jnp.int32, (BLK, BLK), 0)

    def attend(b, at):
        for head in range(heads):
            columns = pl.ds(head * HEAD_DIM, HEAD_DIM)
            query = q[b, :, columns]
            top = jnp.full((BLK, BLK), -1e30, jnp.float32)
            for n in range(slots):
                keys = kpool[slot[b * slots + n], :, columns]
                part = lax.dot_general(query, keys, (((1,), (1,)), ((), ())), preferred_element_type=jnp.float32)
                part = jnp.where(offset <= reach[b * slots + n], part * HEAD_DIM**-0.5, -1e30)
                scores[n] = part
                top = jnp.maximum(top, part)
            top = jnp.max(top, axis=1, keepdims=True)
            total = jnp.zeros((BLK, BLK), jnp.float32)
            blended = jnp.zeros((BLK, HEAD_DIM), jnp.float32)
            for n in range(slots):
                weights = jnp.exp(scores[n] - top)
                total += weights
                values = vpool[slot[b * slots + n], :, columns]
                blended += jnp.dot(weights.astype(jnp.bfloat16), values, preferred_element_type=jnp.float32)
            total = jnp.sum(total, axis=1, keepdims=True)
            attended[at, :, columns] = (blended / total).astype(jnp.bfloat16)

    def cross(g):
        return pltpu.make_async_remote_copy(
            partial.at[g, 0], crossed.at[g], cross_sem.at[0, g], cross_sem.at[1, g], device_id=sibling, device_id_type=MESH
        )

    def travel(n, source, target, peer):
        return pltpu.make_async_remote_copy(
            source, target, sum_send.at[n], sum_recv.at[n], device_id=peer, device_id_type=MESH
        )

    first, second = pl.ds(0, half), pl.ds(half, half)
    travels = [
        travel(0, packed.at[0, first], hop.at[0], right),
        travel(1, packed.at[0, second], hop.at[1], left),
        travel(2, packed.at[1, second], final.at[0, second], right),
        travel(3, packed.at[1, first], final.at[0, first], right),
        travel(4, packed.at[2, first], final.at[1, first], left),
        travel(5, packed.at[2, second], final.at[1, second], left),
    ]

    def add(g, low, more=None):
        @pl.loop(0, half)
        def _(n):
            term = partial[g, 1, low + n].astype(jnp.float32) + crossed[g, low + n].astype(jnp.float32)
            if more is not None:
                term += hop[more, n].astype(jnp.float32)
            packed[g, low + n] = term.astype(jnp.bfloat16)

    for g, steps in enumerate((2, 1, -1, 0)):
        chip = lax.rem(z + steps + chips, chips)

        @pl.loop(0, 2)
        def _(turn):
            attend(chip * 2 + lax.rem(core + 1 + turn, 2), turn)

            @pl.loop(0, pieces)
            def _(n):
                partial[g, turn, n] = jnp.dot(
                    attended[turn], projection[pl.ds(pl.multiple_of(n * width, width), width), :], preferred_element_type=jnp.float32
                ).astype(jnp.bfloat16)

            @pl.when(turn == 0)
            def _():
                cross(g).start()

        cross(g).wait_recv()
        if g == 0:
            add(0, 0)
            travels[0].start()
            add(0, half)
            travels[1].start()
        elif g == 1:
            add(1, half)
            travels[2].start()
        elif g == 2:
            add(2, 0)
            travels[4].start()
            travels[0].wait_recv()
            add(1, 0, 0)
            travels[3].start()
            travels[1].wait_recv()
            add(2, half, 1)
            travels[5].start()

    for low, waits in ((half, (2, 5)), (0, (3, 4))):
        for n in waits:
            travels[n].wait_recv()

        @pl.loop(0, half)
        def _(n):
            at = low + n
            term = partial[3, 1, at].astype(jnp.float32) + crossed[3, at].astype(jnp.float32)
            term += final[0, at].astype(jnp.float32) + final[1, at].astype(jnp.float32)
            out[:, pl.ds(pl.multiple_of(at * wide, wide), wide)] = term.astype(jnp.bfloat16)

    for g in range(chips):
        cross(g).wait_send()
    for copy in travels:
        copy.wait_send()

    @pl.when(me < spans - 1)
    def _():
        for copy in previous(me + 1):
            copy.wait_send()

    @pl.loop(1, spans)
    def _(step):
        @pl.when(me + step < spans)
        def _():
            for copy in listed(me, me + step):
                copy.wait_send()
    for copy in sent:
        copy.wait_send()


def sublayer(tokens, norm_gain, qkv_weight, out_weight, layout, spans, lanes):
    part, features = tokens.shape
    width = qkv_weight.shape[2]
    rows = lanes * part
    slots = 2 + layout.shape[1]
    pick, slot, reach = block_tables(layout, spans)
    weights = jnp.concatenate([qkv_weight, out_weight[None]], axis=0)
    own = rows // BLK
    pool = own + CAP * spans + 1
    whole = (spans, BLK, out_weight.shape[1])
    smem = pl.BlockSpec(memory_space=pltpu.SMEM)
    vmem = pl.BlockSpec(memory_space=pltpu.VMEM)
    bf16 = lambda *shape: pltpu.VMEM(shape, jnp.bfloat16)
    dma = lambda *shape: pltpu.SemaphoreType.DMA(shape)
    side = math.isqrt(spans)
    return pl.pallas_call(
        functools.partial(attend_kernel, side, spans, slots),
        out_shape=jax.ShapeDtypeStruct((BLK, features), jnp.bfloat16),
        in_specs=[smem] * 3 + [vmem] * 3,
        out_specs=vmem,
        scratch_shapes=[
            bf16(rows, features), bf16(rows, features), bf16(4, features, width), bf16(3, own, BLK, width),
            bf16(pool, BLK, width), bf16(pool, BLK, width), bf16(spans * CAP, BLK, width), bf16(spans * CAP, BLK, width),
            pltpu.VMEM((slots, BLK, BLK), jnp.float32), bf16(2, BLK, width),
            bf16(4, 2, *whole), bf16(4, *whole), bf16(3, *whole), bf16(2, spans // 2, *whole[1:]), bf16(2, *whole),
            dma(14), dma(lanes, 2), dma(60), dma(spans, 4), dma(2),
            dma(spans + 1, 2), dma(spans + 1, 2), dma(2, 4), dma(6), dma(6),
        ],
        compiler_params=pltpu.CompilerParams(
            collective_id=0, has_side_effects=True, vmem_limit_bytes=67043328
        ),
    )(pick, slot, reach, tokens, norm_gain[None, :], weights)


def shards(spans, lanes, tokens, norm_gain, qkv_weight, out_weight, layout):
    return sublayer(tokens, norm_gain, qkv_weight, out_weight, layout, spans, lanes)


def solution(mesh):
    placed = (P(("ctx", "fsdp"), None), P(), P(None, "ctx", "fsdp"), P("fsdp", "ctx"), P())
    return jax.shard_map(
        functools.partial(shards, mesh.shape["ctx"], mesh.shape["fsdp"]),
        mesh=mesh, in_specs=placed, out_specs=P(("ctx", "fsdp"), None), check_vma=False,
    )
```

```python
import functools
import math

import jax
import jax.numpy as jnp
from jax import lax
from jax.experimental import pallas as pl
from jax.experimental.pallas import tpu as pltpu
from jax.sharding import PartitionSpec as P

HEAD_DIM = 128
BLK = 128
EPSILON = 1e-05
CAP = 2
MESH = pl.DeviceIdType.MESH


def block_tables(layout, spans):
    me = lax.axis_index("ctx")
    blocks, listed = layout.shape
    own = blocks // spans
    entries = layout.reshape(spans, own * listed)
    home, within = entries // own, entries % own
    mine = home == me
    lowest = jnp.min(jnp.where(mine, within, own - 1), axis=1)
    highest = jnp.max(jnp.where(mine, within, 0), axis=1)
    pick = jnp.stack([lowest, highest], axis=1).reshape(-1)
    rows = lax.dynamic_index_in_dim(entries, me, 0, keepdims=False)
    row_home, row_within = rows // own, rows % own
    same = row_home[:, None] == row_home[None, :]
    low = jnp.min(jnp.where(same, row_within[None, :], own - 1), axis=1)
    far = own + CAP * row_home + jnp.where(row_within == low, 0, 1)
    listed_slot = jnp.where(row_home == me, row_within, far).reshape(own, listed)
    index = jnp.arange(own, dtype=jnp.int32)
    block = me * own + index
    before = jnp.where(index > 0, index - 1, jnp.where(me > 0, own + CAP * spans, 0))
    slot = jnp.concatenate([index[:, None], before[:, None], listed_slot], axis=1)
    gap = block[:, None] - rows.reshape(own, listed)
    before_gap = jnp.where(block > 0, 1, -1)
    reach = jnp.concatenate([jnp.zeros_like(index)[:, None], before_gap[:, None], gap], axis=1) * BLK
    return pick.astype(jnp.int32), slot.reshape(-1).astype(jnp.int32), reach.reshape(-1).astype(jnp.int32)


def gather(side, eps, enter, tokens, gain, weights, rows_all, normed, held, send_t, recv_t, send_w, recv_w, own_sem):
    ctx, lane = lax.axis_index("ctx"), lax.axis_index("fsdp")
    x, y = ctx // side, lax.rem(ctx, side)
    z, core = lane // 2, lax.rem(lane, 2)
    part, width = tokens.shape
    depth = weights.shape[1]
    half, quarter = part // 2, depth // 4

    def shift(at, by):
        return lax.rem(at + by + side, side)

    def along(axis, by):
        if axis == "x":
            return (shift(x, by) * side + y, lane)
        if axis == "y":
            return (x * side + shift(y, by), lane)
        if axis == "z":
            return (ctx, shift(z, by) * 2 + core)
        return (ctx, z * 2 + 1 - core)

    sent = []

    def send_tokens(owner, h, peer, own=False):
        there = rows_all.at[pl.ds(pl.multiple_of(owner * part + h * half, half), half)]
        here = tokens.at[pl.ds(h * half, half)] if own else there
        copy = pltpu.make_async_remote_copy(
            here, there, send_t.at[len([c for c in sent if c[0] == "t"])], recv_t.at[owner, h], device_id=peer, device_id_type=MESH
        )
        copy.start()
        sent.append(("t", copy))

    def wait_tokens(owner, h):
        there = rows_all.at[pl.ds(pl.multiple_of(owner * part + h * half, half), half)]
        pltpu.make_async_remote_copy(
            there, there, send_t.at[0], recv_t.at[owner, h], device_id=along("core", 1), device_id_type=MESH
        ).wait_recv()

    def piece_of(owner, p):
        return held.at[:, pl.ds(pl.multiple_of(owner * depth + p * quarter, quarter), quarter)]

    def send_weights(owner, p, peer, own=False):
        there = piece_of(owner, p)
        here = weights.at[:, pl.ds(p * quarter, quarter)] if own else there
        copy = pltpu.make_async_remote_copy(
            here, there, send_w.at[len([c for c in sent if c[0] == "w"])], recv_w.at[owner, p], device_id=peer, device_id_type=MESH
        )
        copy.start()
        sent.append(("w", copy))

    def wait_weights(owner, p):
        pltpu.make_async_remote_copy(
            piece_of(owner, p), piece_of(owner, p), send_w.at[0], recv_w.at[owner, p], device_id=along("core", 1), device_id_type=MESH
        ).wait_recv()

    def normalize_rows(owner):
        @pl.loop(0, part // 16)
        def _(n):
            at = pl.ds(pl.multiple_of(owner * part + n * 16, 16), 16)
            features = rows_all[at, :].astype(jnp.float32)
            mean_square = jnp.mean(features * features, axis=-1, keepdims=True)
            normed[at, :] = (features * lax.rsqrt(mean_square + eps) * gain[...]).astype(jnp.bfloat16)

    keep = [
        pltpu.make_async_copy(tokens, rows_all.at[pl.ds(pl.multiple_of(lane * part, part), part)], own_sem.at[0]),
        pltpu.make_async_copy(weights, held.at[:, pl.ds(pl.multiple_of(ctx * depth, depth), depth)], own_sem.at[1]),
    ]
    for copy in keep:
        copy.start()
    enter()

    routes = (("x", "y", 0), ("y", "x", 2))

    def owner_at(axis, by, other=0):
        if axis == "x":
            return shift(x, by) * side + shift(y, other)
        return shift(x, other) * side + shift(y, by)

    right, left, sibling = along("z", 1), along("z", -1), along("core", 1)
    lane_at = lambda by, flip=0: shift(z, by) * 2 + (1 - core if flip else core)
    send_tokens(lane, 0, right, own=True)
    send_tokens(lane, 1, left, own=True)
    for first, second, p in routes:
        send_weights(ctx, p, along(first, 1), own=True)
        send_weights(ctx, p + 1, along(first, -1), own=True)
        send_weights(ctx, p + 1, along(first, 1), own=True)
        send_weights(ctx, p, along(first, -1), own=True)
    send_tokens(lane, 1, right, own=True)
    send_tokens(lane, 0, left, own=True)
    for h in range(2):
        send_tokens(lane, h, sibling, own=True)
    for first, second, p in routes:
        send_weights(ctx, p, along(second, 1), own=True)
        send_weights(ctx, p + 1, along(second, -1), own=True)
        send_weights(ctx, p + 1, along(second, 1), own=True)
        send_weights(ctx, p, along(second, -1), own=True)
    for copy in keep:
        copy.wait()
    normalize_rows(lane)

    def spread(owner, p, axis):
        send_weights(owner, p, along(axis, 1))
        send_weights(owner, p, along(axis, -1))

    for first, second, p in routes:
        wait_weights(owner_at(first, -1), p)
        send_weights(owner_at(first, -1), p, along(first, 1))
        wait_weights(owner_at(first, 1), p + 1)
        send_weights(owner_at(first, 1), p + 1, along(first, -1))
    for first, second, p in routes:
        spread(owner_at(first, -1), p, second)
        spread(owner_at(first, 1), p + 1, second)
    for first, second, p in routes:
        wait_weights(owner_at(first, -1), p + 1)
        spread(owner_at(first, -1), p + 1, second)
        wait_weights(owner_at(first, 1), p)
        spread(owner_at(first, 1), p, second)

    def relay(by):
        for first, second, p in routes:
            owner = owner_at(first, by, -1)
            wait_weights(owner, p)
            send_weights(owner, p, along(second, 1))
            owner = owner_at(first, by, 1)
            wait_weights(owner, p + 1)
            send_weights(owner, p + 1, along(second, -1))

    for first, second, p in routes:
        for q in (p, p + 1):
            wait_weights(owner_at(first, 2), q)
            spread(owner_at(first, 2), q, second)
    relay(0)
    wait_tokens(lane_at(-1), 0)
    send_tokens(lane_at(-1), 0, right)
    send_tokens(lane_at(-1), 0, sibling)
    wait_tokens(lane_at(1), 1)
    send_tokens(lane_at(1), 1, left)
    send_tokens(lane_at(1), 1, sibling)
    relay(-1)
    relay(1)
    for h in range(2):
        wait_tokens(lane_at(0, 1), h)
    normalize_rows(lane_at(0, 1))
    wait_tokens(lane_at(-1), 1)
    send_tokens(lane_at(-1), 1, sibling)
    wait_tokens(lane_at(1), 0)
    send_tokens(lane_at(1), 0, sibling)
    normalize_rows(lane_at(-1))
    normalize_rows(lane_at(1))
    relay(2)
    for by in (-1, 1):
        for h in range(2):
            wait_tokens(lane_at(by, 1), h)
        normalize_rows(lane_at(by, 1))
    for h in range(2):
        wait_tokens(lane_at(2), h)
        send_tokens(lane_at(2), h, sibling)
    normalize_rows(lane_at(2))
    for first, second, p in routes:
        for by in (0, -1, 1, 2):
            wait_weights(owner_at(first, by, -1), p + 1)
            wait_weights(owner_at(first, by, 1), p)
            wait_weights(owner_at(first, by, 2), p)
            wait_weights(owner_at(first, by, 2), p + 1)
    for h in range(2):
        wait_tokens(lane_at(2, 1), h)
    normalize_rows(lane_at(2, 1))

    return [copy for _, copy in sent]


def attend_kernel(
    side, spans, slots, pick, slot, reach, tokens, gain, weights, out, rows_all, normed, held, projected,
    kpool, vpool, kstage, vstage, scores, attended, partial, crossed, packed, hop, final,
    send_t, recv_t, send_w, recv_w, own_sem, send_sem, recv_sem, cross_sem, sum_send, sum_recv,
):
    me, lane = lax.axis_index("ctx"), lax.axis_index("fsdp")
    q, k, v = (projected.at[which] for which in range(3))
    z, core = lane // 2, lax.rem(lane, 2)
    chips = 4
    pieces, wide = spans, held.shape[2]
    projection = held.at[3]
    half = pieces // 2
    right = (me, lax.rem(z + 1, chips) * 2 + core)
    left = (me, lax.rem(z + chips - 1, chips) * 2 + core)
    sibling = (me, z * 2 + 1 - core)
    own = q.shape[0]
    width = q.shape[2]
    heads = width // HEAD_DIM
    barrier = pltpu.get_barrier_semaphore()

    @pl.loop(1, spans)
    def _(step):
        peer = lax.rem(me + step, spans)
        pl.semaphore_signal(barrier, inc=1, device_id=(peer, lane), device_id_type=MESH)

    for peer in (right, left, sibling):
        pl.semaphore_signal(barrier, inc=1, device_id=peer, device_id_type=MESH)

    sent = gather(
        side, EPSILON, lambda: pl.semaphore_wait(barrier, spans + 2), tokens, gain, weights,
        rows_all, normed, held, send_t, recv_t, send_w, recv_w, own_sem,
    )
    tile = 2 * BLK

    def project(which):
        @pl.loop(0, normed.shape[0] // tile)
        def _(n):
            rows = normed[pl.ds(pl.multiple_of(n * tile, tile), tile), :]
            product = jnp.dot(rows, held[which], preferred_element_type=jnp.float32)
            projected[which, pl.ds(2 * n, 2)] = product.astype(jnp.bfloat16).reshape(2, BLK, width)

    project(1)
    project(2)
    keep = [
        pltpu.make_async_copy(k, kpool.at[pl.ds(0, own)], own_sem.at[0]),
        pltpu.make_async_copy(v, vpool.at[pl.ds(0, own)], own_sem.at[1]),
    ]
    for copy in keep:
        copy.start()

    @pl.loop(0, spans * CAP)
    def _(n):
        kstage[n] = k[pick[n]]
        vstage[n] = v[pick[n]]

    def listed(src, dst):
        there = pl.ds(own + CAP * src, CAP)
        return [
            pltpu.make_async_remote_copy(
                stage.at[pl.ds(CAP * dst, CAP)], pool.at[there],
                send_sem.at[dst, j], recv_sem.at[src, j], device_id=(dst, lane), device_id_type=MESH,
            )
            for j, (stage, pool) in enumerate(((kstage, kpool), (vstage, vpool)))
        ]

    def previous(dst):
        there = own + CAP * spans
        return [
            pltpu.make_async_remote_copy(
                mine.at[own - 1], pool.at[there],
                send_sem.at[spans, j], recv_sem.at[spans, j], device_id=(dst, lane), device_id_type=MESH,
            )
            for j, (mine, pool) in enumerate(((k, kpool), (v, vpool)))
        ]

    @pl.when(me < spans - 1)
    def _():
        for copy in previous(me + 1):
            copy.start()

    x, y = me // side, lax.rem(me, side)
    for by in (2, 3, 1, 0):

        @pl.loop(0, side)
        def _(step):
            dst = (x + by) * side + lax.rem(y + step, side)

            @pl.when((x + by < side) & (dst > me))
            def _():
                for copy in listed(me, dst):
                    copy.start()

    project(0)
    for copy in keep:
        copy.wait()

    @pl.when(me > 0)
    def _():
        for copy in previous(me):
            copy.wait_recv()

    @pl.loop(1, spans)
    def _(step):
        @pl.when(me >= step)
        def _():
            for copy in listed(me - step, me):
                copy.wait_recv()

    column = lax.broadcasted_iota(jnp.int32, (BLK, 2 * BLK), 1)
    late = column >= BLK
    offset = lax.rem(column, BLK) - lax.broadcasted_iota(jnp.int32, (BLK, 2 * BLK), 0)

    def attend(b, at):
        for head in range(heads):
            columns = pl.ds(head * HEAD_DIM, HEAD_DIM)
            query = q[b, :, columns]
            pair = lambda pool, n: jnp.concatenate(
                [pool[slot[b * slots + n], :, columns], pool[slot[b * slots + n + 1], :, columns]], axis=0
            )
            top = jnp.full((BLK, 2 * BLK), -1e30, jnp.float32)
            for n in range(0, slots, 2):
                part = lax.dot_general(
                    query, pair(kpool, n), (((1,), (1,)), ((), ())), preferred_element_type=jnp.float32
                )
                limit = jnp.where(late, reach[b * slots + n + 1], reach[b * slots + n])
                part = jnp.where(offset <= limit, part, -1e30)
                scores[n // 2] = part
                top = jnp.maximum(top, part)
            top = jnp.max(top, axis=1, keepdims=True)
            total = jnp.zeros((BLK, 2 * BLK), jnp.float32)
            blended = jnp.zeros((BLK, HEAD_DIM), jnp.float32)
            for n in range(0, slots, 2):
                terms = jnp.exp((scores[n // 2] - top) * HEAD_DIM**-0.5)
                total += terms
                blended += jnp.dot(terms.astype(jnp.bfloat16), pair(vpool, n), preferred_element_type=jnp.float32)
            total = jnp.sum(total, axis=1, keepdims=True)
            attended[at, :, columns] = (blended / total).astype(jnp.bfloat16)

    def cross(g):
        return pltpu.make_async_remote_copy(
            partial.at[g, 0], crossed.at[g], cross_sem.at[0, g], cross_sem.at[1, g], device_id=sibling, device_id_type=MESH
        )

    def travel(n, source, target, peer):
        return pltpu.make_async_remote_copy(
            source, target, sum_send.at[n], sum_recv.at[n], device_id=peer, device_id_type=MESH
        )

    first, second = pl.ds(0, half), pl.ds(half, half)
    travels = [
        travel(0, packed.at[0, first], hop.at[0], right),
        travel(1, packed.at[0, second], hop.at[1], left),
        travel(2, packed.at[1, second], final.at[0, second], right),
        travel(3, packed.at[1, first], final.at[0, first], right),
        travel(4, packed.at[2, first], final.at[1, first], left),
        travel(5, packed.at[2, second], final.at[1, second], left),
    ]

    def add(g, low, more=None):
        @pl.loop(0, half)
        def _(n):
            term = partial[g, 1, low + n].astype(jnp.float32) + crossed[g, low + n].astype(jnp.float32)
            if more is not None:
                term += hop[more, n].astype(jnp.float32)
            packed[g, low + n] = term.astype(jnp.bfloat16)

    for g, steps in enumerate((2, 1, -1, 0)):
        chip = lax.rem(z + steps + chips, chips)

        @pl.loop(0, 2)
        def _(turn):
            attend(chip * 2 + lax.rem(core + 1 + turn, 2), turn)

            @pl.loop(0, pieces)
            def _(n):
                partial[g, turn, n] = jnp.dot(
                    attended[turn], projection[pl.ds(pl.multiple_of(n * width, width), width), :], preferred_element_type=jnp.float32
                ).astype(jnp.bfloat16)

            @pl.when(turn == 0)
            def _():
                cross(g).start()

        cross(g).wait_recv()
        if g == 0:
            add(0, 0)
            travels[0].start()
            add(0, half)
            travels[1].start()
        elif g == 1:
            add(1, half)
            travels[2].start()
        elif g == 2:
            add(2, 0)
            travels[4].start()
            travels[0].wait_recv()
            add(1, 0, 0)
            travels[3].start()
            travels[1].wait_recv()
            add(2, half, 1)
            travels[5].start()

    for low, waits in ((half, (2, 5)), (0, (3, 4))):
        for n in waits:
            travels[n].wait_recv()

        @pl.loop(0, half)
        def _(n):
            at = low + n
            term = partial[3, 1, at].astype(jnp.float32) + crossed[3, at].astype(jnp.float32)
            term += final[0, at].astype(jnp.float32) + final[1, at].astype(jnp.float32)
            out[:, pl.ds(pl.multiple_of(at * wide, wide), wide)] = term.astype(jnp.bfloat16)

    for g in range(chips):
        cross(g).wait_send()
    for copy in travels:
        copy.wait_send()

    @pl.when(me < spans - 1)
    def _():
        for copy in previous(me + 1):
            copy.wait_send()

    @pl.loop(1, spans)
    def _(step):
        @pl.when(me + step < spans)
        def _():
            for copy in listed(me, me + step):
                copy.wait_send()
    for copy in sent:
        copy.wait_send()


def sublayer(tokens, norm_gain, qkv_weight, out_weight, layout, spans, lanes):
    part, features = tokens.shape
    width = qkv_weight.shape[2]
    rows = lanes * part
    slots = 2 + layout.shape[1]
    pick, slot, reach = block_tables(layout, spans)
    weights = jnp.concatenate([qkv_weight, out_weight[None]], axis=0)
    own = rows // BLK
    pool = own + CAP * spans + 1
    whole = (spans, BLK, out_weight.shape[1])
    smem = pl.BlockSpec(memory_space=pltpu.SMEM)
    vmem = pl.BlockSpec(memory_space=pltpu.VMEM)
    bf16 = lambda *shape: pltpu.VMEM(shape, jnp.bfloat16)
    dma = lambda *shape: pltpu.SemaphoreType.DMA(shape)
    side = math.isqrt(spans)
    return pl.pallas_call(
        functools.partial(attend_kernel, side, spans, slots),
        out_shape=jax.ShapeDtypeStruct((BLK, features), jnp.bfloat16),
        in_specs=[smem] * 3 + [vmem] * 3,
        out_specs=vmem,
        scratch_shapes=[
            bf16(rows, features), bf16(rows, features), bf16(4, features, width), bf16(3, own, BLK, width),
            bf16(pool, BLK, width), bf16(pool, BLK, width), bf16(spans * CAP, BLK, width), bf16(spans * CAP, BLK, width),
            pltpu.VMEM((slots // 2, BLK, 2 * BLK), jnp.float32), bf16(2, BLK, width),
            bf16(4, 2, *whole), bf16(4, *whole), bf16(3, *whole), bf16(2, spans // 2, *whole[1:]), bf16(2, *whole),
            dma(14), dma(lanes, 2), dma(60), dma(spans, 4), dma(2),
            dma(spans + 1, 2), dma(spans + 1, 2), dma(2, 4), dma(6), dma(6),
        ],
        compiler_params=pltpu.CompilerParams(
            collective_id=0, has_side_effects=True, vmem_limit_bytes=67043328
        ),
    )(pick, slot, reach, tokens, norm_gain[None, :], weights)


def shards(spans, lanes, tokens, norm_gain, qkv_weight, out_weight, layout):
    return sublayer(tokens, norm_gain, qkv_weight, out_weight, layout, spans, lanes)


def solution(mesh):
    placed = (P(("ctx", "fsdp"), None), P(), P(None, "ctx", "fsdp"), P("fsdp", "ctx"), P())
    return jax.shard_map(
        functools.partial(shards, mesh.shape["ctx"], mesh.shape["fsdp"]),
        mesh=mesh, in_specs=placed, out_specs=P(("ctx", "fsdp"), None), check_vma=False,
    )
```

```python
import functools
import math

import jax
import jax.numpy as jnp
from jax import lax
from jax.experimental import pallas as pl
from jax.experimental.pallas import tpu as pltpu
from jax.sharding import PartitionSpec as P

HEAD_DIM = 128
BLK = 128
EPSILON = 1e-05
CAP = 2
MESH = pl.DeviceIdType.MESH


def block_tables(layout, spans):
    me = lax.axis_index("ctx")
    blocks, listed = layout.shape
    own = blocks // spans
    entries = layout.reshape(spans, own * listed)
    home, within = entries // own, entries % own
    mine = home == me
    lowest = jnp.min(jnp.where(mine, within, own - 1), axis=1)
    highest = jnp.max(jnp.where(mine, within, 0), axis=1)
    pick = jnp.stack([lowest, highest], axis=1).reshape(-1)
    rows = lax.dynamic_index_in_dim(entries, me, 0, keepdims=False)
    row_home, row_within = rows // own, rows % own
    same = row_home[:, None] == row_home[None, :]
    low = jnp.min(jnp.where(same, row_within[None, :], own - 1), axis=1)
    far = own + CAP * row_home + jnp.where(row_within == low, 0, 1)
    listed_slot = jnp.where(row_home == me, row_within, far).reshape(own, listed)
    index = jnp.arange(own, dtype=jnp.int32)
    block = me * own + index
    before = jnp.where(index > 0, index - 1, jnp.where(me > 0, own + CAP * spans, 0))
    slot = jnp.concatenate([index[:, None], before[:, None], listed_slot], axis=1)
    gap = block[:, None] - rows.reshape(own, listed)
    before_gap = jnp.where(block > 0, 1, -1)
    reach = jnp.concatenate([jnp.zeros_like(index)[:, None], before_gap[:, None], gap], axis=1) * BLK
    return pick.astype(jnp.int32), slot.reshape(-1).astype(jnp.int32), reach.reshape(-1).astype(jnp.int32)


def gather(side, eps, enter, tokens, gain, weights, out_weight, rows_all, normed, held, projection, send_t, recv_t, send_w, recv_w, own_sem):
    ctx, lane = lax.axis_index("ctx"), lax.axis_index("fsdp")
    x, y = ctx // side, lax.rem(ctx, side)
    z, core = lane // 2, lax.rem(lane, 2)
    part, width = tokens.shape
    depth = weights.shape[1]
    half, quarter = part // 2, depth // 4

    def shift(at, by):
        return lax.rem(at + by + side, side)

    def along(axis, by):
        if axis == "x":
            return (shift(x, by) * side + y, lane)
        if axis == "y":
            return (x * side + shift(y, by), lane)
        if axis == "z":
            return (ctx, shift(z, by) * 2 + core)
        return (ctx, z * 2 + 1 - core)

    sent = []

    def send_tokens(owner, h, peer, own=False):
        there = rows_all.at[pl.ds(pl.multiple_of(owner * part + h * half, half), half)]
        here = tokens.at[pl.ds(h * half, half)] if own else there
        copy = pltpu.make_async_remote_copy(
            here, there, send_t.at[len([c for c in sent if c[0] == "t"])], recv_t.at[owner, h], device_id=peer, device_id_type=MESH
        )
        copy.start()
        sent.append(("t", copy))

    def wait_tokens(owner, h):
        there = rows_all.at[pl.ds(pl.multiple_of(owner * part + h * half, half), half)]
        pltpu.make_async_remote_copy(
            there, there, send_t.at[0], recv_t.at[owner, h], device_id=along("core", 1), device_id_type=MESH
        ).wait_recv()

    def rows_of(ref, start, count):
        return ref.at[:, pl.ds(start, count)] if len(ref.shape) == 3 else ref.at[pl.ds(start, count)]

    families = ((weights, held), (out_weight, projection))

    def piece_of(owner, p, kind):
        return rows_of(families[kind][1], pl.multiple_of(owner * depth + p * quarter, quarter), quarter)

    def send_weights(owner, p, peer, kind=0, own=False):
        there = piece_of(owner, p, kind)
        here = rows_of(families[kind][0], p * quarter, quarter) if own else there
        copy = pltpu.make_async_remote_copy(
            here, there, send_w.at[kind, len([c for c in sent if c[0] == kind])], recv_w.at[kind, owner, p],
            device_id=peer, device_id_type=MESH,
        )
        copy.start()
        sent.append((kind, copy))

    def wait_weights(owner, p, kind=0):
        piece = piece_of(owner, p, kind)
        pltpu.make_async_remote_copy(
            piece, piece, send_w.at[kind, 0], recv_w.at[kind, owner, p], device_id=along("core", 1), device_id_type=MESH
        ).wait_recv()

    def normalize_rows(owner):
        @pl.loop(0, part // 16)
        def _(n):
            at = pl.ds(pl.multiple_of(owner * part + n * 16, 16), 16)
            features = rows_all[at, :].astype(jnp.float32)
            mean_square = jnp.mean(features * features, axis=-1, keepdims=True)
            normed[at, :] = (features * lax.rsqrt(mean_square + eps) * gain[...]).astype(jnp.bfloat16)

    keep = [
        pltpu.make_async_copy(tokens, rows_all.at[pl.ds(pl.multiple_of(lane * part, part), part)], own_sem.at[0]),
        pltpu.make_async_copy(weights, held.at[:, pl.ds(pl.multiple_of(ctx * depth, depth), depth)], own_sem.at[1]),
        pltpu.make_async_copy(out_weight, projection.at[pl.ds(pl.multiple_of(ctx * depth, depth), depth)], own_sem.at[2]),
    ]
    for copy in keep:
        copy.start()
    enter()

    routes = (("x", "y", 0), ("y", "x", 2))

    def owner_at(axis, by, other=0):
        if axis == "x":
            return shift(x, by) * side + shift(y, other)
        return shift(x, other) * side + shift(y, by)

    right, left, sibling = along("z", 1), along("z", -1), along("core", 1)
    lane_at = lambda by, flip=0: shift(z, by) * 2 + (1 - core if flip else core)
    send_tokens(lane, 0, right, own=True)
    send_tokens(lane, 1, left, own=True)

    def send_own(turn, kind=0):
        for route in routes:
            axis, p = route[turn], route[2]
            send_weights(ctx, p, along(axis, 1), kind, own=True)
            send_weights(ctx, p + 1, along(axis, -1), kind, own=True)
            send_weights(ctx, p + 1, along(axis, 1), kind, own=True)
            send_weights(ctx, p, along(axis, -1), kind, own=True)

    send_own(0)
    send_tokens(lane, 1, right, own=True)
    send_tokens(lane, 0, left, own=True)
    for h in range(2):
        send_tokens(lane, h, sibling, own=True)
    send_own(1)
    for copy in keep:
        copy.wait()
    normalize_rows(lane)

    def spread(owner, p, axis, kind):
        send_weights(owner, p, along(axis, 1), kind)
        send_weights(owner, p, along(axis, -1), kind)

    def turn_corner(kind=0):
        for first, second, p in routes:
            wait_weights(owner_at(first, -1), p, kind)
            send_weights(owner_at(first, -1), p, along(first, 1), kind)
            wait_weights(owner_at(first, 1), p + 1, kind)
            send_weights(owner_at(first, 1), p + 1, along(first, -1), kind)
        for first, second, p in routes:
            spread(owner_at(first, -1), p, second, kind)
            spread(owner_at(first, 1), p + 1, second, kind)
        for first, second, p in routes:
            wait_weights(owner_at(first, -1), p + 1, kind)
            spread(owner_at(first, -1), p + 1, second, kind)
            wait_weights(owner_at(first, 1), p, kind)
            spread(owner_at(first, 1), p, second, kind)
        for first, second, p in routes:
            for q in (p, p + 1):
                wait_weights(owner_at(first, 2), q, kind)
                spread(owner_at(first, 2), q, second, kind)

    def relay(by, kind=0):
        for first, second, p in routes:
            owner = owner_at(first, by, -1)
            wait_weights(owner, p, kind)
            send_weights(owner, p, along(second, 1), kind)
            owner = owner_at(first, by, 1)
            wait_weights(owner, p + 1, kind)
            send_weights(owner, p + 1, along(second, -1), kind)

    def finish(kind=0):
        for first, second, p in routes:
            for by in (0, -1, 1, 2):
                wait_weights(owner_at(first, by, -1), p + 1, kind)
                wait_weights(owner_at(first, by, 1), p, kind)
                wait_weights(owner_at(first, by, 2), p, kind)
                wait_weights(owner_at(first, by, 2), p + 1, kind)

    turn_corner()
    relay(0)
    wait_tokens(lane_at(-1), 0)
    send_tokens(lane_at(-1), 0, right)
    send_tokens(lane_at(-1), 0, sibling)
    wait_tokens(lane_at(1), 1)
    send_tokens(lane_at(1), 1, left)
    send_tokens(lane_at(1), 1, sibling)
    relay(-1)
    relay(1)
    for h in range(2):
        wait_tokens(lane_at(0, 1), h)
    normalize_rows(lane_at(0, 1))
    wait_tokens(lane_at(-1), 1)
    send_tokens(lane_at(-1), 1, sibling)
    wait_tokens(lane_at(1), 0)
    send_tokens(lane_at(1), 0, sibling)
    normalize_rows(lane_at(-1))
    normalize_rows(lane_at(1))
    relay(2)
    send_own(0, 1)
    send_own(1, 1)
    for by in (-1, 1):
        for h in range(2):
            wait_tokens(lane_at(by, 1), h)
        normalize_rows(lane_at(by, 1))
    for h in range(2):
        wait_tokens(lane_at(2), h)
        send_tokens(lane_at(2), h, sibling)
    normalize_rows(lane_at(2))
    finish()
    turn_corner(1)
    for h in range(2):
        wait_tokens(lane_at(2, 1), h)
    normalize_rows(lane_at(2, 1))

    return sent, lambda *steps: [relay(by, 1) for by in steps], lambda: finish(1)


def attend_kernel(
    side, spans, slots, pick, slot, reach, tokens, gain, weights, out_weight, out, rows_all, normed, held, projection, projected,
    kpool, vpool, kstage, vstage, scores, attended, partial, crossed, packed, hop, final,
    send_t, recv_t, send_w, recv_w, own_sem, send_sem, recv_sem, cross_sem, sum_send, sum_recv,
):
    me, lane = lax.axis_index("ctx"), lax.axis_index("fsdp")
    q, k, v = (projected.at[which] for which in range(3))
    z, core = lane // 2, lax.rem(lane, 2)
    chips = 4
    pieces, wide = spans, held.shape[2]
    half = pieces // 2
    right = (me, lax.rem(z + 1, chips) * 2 + core)
    left = (me, lax.rem(z + chips - 1, chips) * 2 + core)
    sibling = (me, z * 2 + 1 - core)
    own = q.shape[0]
    width = q.shape[2]
    heads = width // HEAD_DIM
    barrier = pltpu.get_barrier_semaphore()

    @pl.loop(1, spans)
    def _(step):
        peer = lax.rem(me + step, spans)
        pl.semaphore_signal(barrier, inc=1, device_id=(peer, lane), device_id_type=MESH)

    for peer in (right, left, sibling):
        pl.semaphore_signal(barrier, inc=1, device_id=peer, device_id_type=MESH)

    sent, relay_projection, finish_projection = gather(
        side, EPSILON, lambda: pl.semaphore_wait(barrier, spans + 2), tokens, gain, weights, out_weight,
        rows_all, normed, held, projection, send_t, recv_t, send_w, recv_w, own_sem,
    )
    tile = 2 * BLK

    def project(which):
        @pl.loop(0, normed.shape[0] // tile)
        def _(n):
            rows = normed[pl.ds(pl.multiple_of(n * tile, tile), tile), :]
            product = jnp.dot(rows, held[which], preferred_element_type=jnp.float32)
            projected[which, pl.ds(2 * n, 2)] = product.astype(jnp.bfloat16).reshape(2, BLK, width)

    project(1)
    relay_projection(0, -1, 1)
    project(2)
    relay_projection(2)
    keep = [
        pltpu.make_async_copy(k, kpool.at[pl.ds(0, own)], own_sem.at[0]),
        pltpu.make_async_copy(v, vpool.at[pl.ds(0, own)], own_sem.at[1]),
    ]
    for copy in keep:
        copy.start()

    @pl.loop(0, spans * CAP)
    def _(n):
        kstage[n] = k[pick[n]]
        vstage[n] = v[pick[n]]

    def listed(src, dst):
        there = pl.ds(own + CAP * src, CAP)
        return [
            pltpu.make_async_remote_copy(
                stage.at[pl.ds(CAP * dst, CAP)], pool.at[there],
                send_sem.at[dst, j], recv_sem.at[src, j], device_id=(dst, lane), device_id_type=MESH,
            )
            for j, (stage, pool) in enumerate(((kstage, kpool), (vstage, vpool)))
        ]

    def previous(dst):
        there = own + CAP * spans
        return [
            pltpu.make_async_remote_copy(
                mine.at[own - 1], pool.at[there],
                send_sem.at[spans, j], recv_sem.at[spans, j], device_id=(dst, lane), device_id_type=MESH,
            )
            for j, (mine, pool) in enumerate(((k, kpool), (v, vpool)))
        ]

    @pl.when(me < spans - 1)
    def _():
        for copy in previous(me + 1):
            copy.start()

    x, y = me // side, lax.rem(me, side)
    for by in (2, 3, 1, 0):

        @pl.loop(0, side)
        def _(step):
            dst = (x + by) * side + lax.rem(y + step, side)

            @pl.when((x + by < side) & (dst > me))
            def _():
                for copy in listed(me, dst):
                    copy.start()

    project(0)
    finish_projection()
    for copy in keep:
        copy.wait()

    @pl.when(me > 0)
    def _():
        for copy in previous(me):
            copy.wait_recv()

    @pl.loop(1, spans)
    def _(step):
        @pl.when(me >= step)
        def _():
            for copy in listed(me - step, me):
                copy.wait_recv()

    column = lax.broadcasted_iota(jnp.int32, (BLK, 2 * BLK), 1)
    late = column >= BLK
    offset = lax.rem(column, BLK) - lax.broadcasted_iota(jnp.int32, (BLK, 2 * BLK), 0)

    def attend(b, at):
        for head in range(heads):
            columns = pl.ds(head * HEAD_DIM, HEAD_DIM)
            query = q[b, :, columns]
            pair = lambda pool, n: jnp.concatenate(
                [pool[slot[b * slots + n], :, columns], pool[slot[b * slots + n + 1], :, columns]], axis=0
            )
            top = jnp.full((BLK, 2 * BLK), -1e30, jnp.float32)
            for n in range(0, slots, 2):
                part = lax.dot_general(
                    query, pair(kpool, n), (((1,), (1,)), ((), ())), preferred_element_type=jnp.float32
                )
                limit = jnp.where(late, reach[b * slots + n + 1], reach[b * slots + n])
                part = jnp.where(offset <= limit, part, -1e30)
                scores[n // 2] = part
                top = jnp.maximum(top, part)
            top = jnp.max(top, axis=1, keepdims=True)
            total = jnp.zeros((BLK, 2 * BLK), jnp.float32)
            blended = jnp.zeros((BLK, HEAD_DIM), jnp.float32)
            for n in range(0, slots, 2):
                terms = jnp.exp((scores[n // 2] - top) * HEAD_DIM**-0.5)
                total += terms
                blended += jnp.dot(terms.astype(jnp.bfloat16), pair(vpool, n), preferred_element_type=jnp.float32)
            total = jnp.sum(total, axis=1, keepdims=True)
            attended[at, :, columns] = (blended / total).astype(jnp.bfloat16)

    def cross(g):
        return pltpu.make_async_remote_copy(
            partial.at[g, 0], crossed.at[g], cross_sem.at[0, g], cross_sem.at[1, g], device_id=sibling, device_id_type=MESH
        )

    def travel(n, source, target, peer):
        return pltpu.make_async_remote_copy(
            source, target, sum_send.at[n], sum_recv.at[n], device_id=peer, device_id_type=MESH
        )

    first, second = pl.ds(0, half), pl.ds(half, half)
    travels = [
        travel(0, packed.at[0, first], hop.at[0], right),
        travel(1, packed.at[0, second], hop.at[1], left),
        travel(2, packed.at[1, second], final.at[0, second], right),
        travel(3, packed.at[1, first], final.at[0, first], right),
        travel(4, packed.at[2, first], final.at[1, first], left),
        travel(5, packed.at[2, second], final.at[1, second], left),
    ]

    def add(g, low, more=None):
        @pl.loop(0, half)
        def _(n):
            term = partial[g, 1, low + n].astype(jnp.float32) + crossed[g, low + n].astype(jnp.float32)
            if more is not None:
                term += hop[more, n].astype(jnp.float32)
            packed[g, low + n] = term.astype(jnp.bfloat16)

    for g, steps in enumerate((2, 1, -1, 0)):
        chip = lax.rem(z + steps + chips, chips)

        @pl.loop(0, 2)
        def _(turn):
            attend(chip * 2 + lax.rem(core + 1 + turn, 2), turn)

            @pl.loop(0, pieces)
            def _(n):
                partial[g, turn, n] = jnp.dot(
                    attended[turn], projection[pl.ds(pl.multiple_of(n * width, width), width), :], preferred_element_type=jnp.float32
                ).astype(jnp.bfloat16)

            @pl.when(turn == 0)
            def _():
                cross(g).start()

        cross(g).wait_recv()
        if g == 0:
            add(0, 0)
            travels[0].start()
            add(0, half)
            travels[1].start()
        elif g == 1:
            add(1, half)
            travels[2].start()
        elif g == 2:
            add(2, 0)
            travels[4].start()
            travels[0].wait_recv()
            add(1, 0, 0)
            travels[3].start()
            travels[1].wait_recv()
            add(2, half, 1)
            travels[5].start()

    for low, waits in ((half, (2, 5)), (0, (3, 4))):
        for n in waits:
            travels[n].wait_recv()

        @pl.loop(0, half)
        def _(n):
            at = low + n
            term = partial[3, 1, at].astype(jnp.float32) + crossed[3, at].astype(jnp.float32)
            term += final[0, at].astype(jnp.float32) + final[1, at].astype(jnp.float32)
            out[:, pl.ds(pl.multiple_of(at * wide, wide), wide)] = term.astype(jnp.bfloat16)

    for g in range(chips):
        cross(g).wait_send()
    for copy in travels:
        copy.wait_send()

    @pl.when(me < spans - 1)
    def _():
        for copy in previous(me + 1):
            copy.wait_send()

    @pl.loop(1, spans)
    def _(step):
        @pl.when(me + step < spans)
        def _():
            for copy in listed(me, me + step):
                copy.wait_send()
    for _, copy in sent:
        copy.wait_send()


def sublayer(tokens, norm_gain, qkv_weight, out_weight, layout, spans, lanes):
    part, features = tokens.shape
    width = qkv_weight.shape[2]
    rows = lanes * part
    slots = 2 + layout.shape[1]
    pick, slot, reach = block_tables(layout, spans)
    own = rows // BLK
    pool = own + CAP * spans + 1
    whole = (spans, BLK, out_weight.shape[1])
    smem = pl.BlockSpec(memory_space=pltpu.SMEM)
    vmem = pl.BlockSpec(memory_space=pltpu.VMEM)
    bf16 = lambda *shape: pltpu.VMEM(shape, jnp.bfloat16)
    dma = lambda *shape: pltpu.SemaphoreType.DMA(shape)
    side = math.isqrt(spans)
    return pl.pallas_call(
        functools.partial(attend_kernel, side, spans, slots),
        out_shape=jax.ShapeDtypeStruct((BLK, features), jnp.bfloat16),
        in_specs=[smem] * 3 + [vmem] * 4,
        out_specs=vmem,
        scratch_shapes=[
            bf16(rows, features), bf16(rows, features), bf16(3, features, width), bf16(features, width),
            bf16(3, own, BLK, width),
            bf16(pool, BLK, width), bf16(pool, BLK, width), bf16(spans * CAP, BLK, width), bf16(spans * CAP, BLK, width),
            pltpu.VMEM((slots // 2, BLK, 2 * BLK), jnp.float32), bf16(2, BLK, width),
            bf16(4, 2, *whole), bf16(4, *whole), bf16(3, *whole), bf16(2, spans // 2, *whole[1:]), bf16(2, *whole),
            dma(14), dma(lanes, 2), dma(2, 60), dma(2, spans, 4), dma(3),
            dma(spans + 1, 2), dma(spans + 1, 2), dma(2, 4), dma(6), dma(6),
        ],
        compiler_params=pltpu.CompilerParams(
            collective_id=0, has_side_effects=True, vmem_limit_bytes=67043328
        ),
    )(pick, slot, reach, tokens, norm_gain[None, :], qkv_weight, out_weight)


def shards(spans, lanes, tokens, norm_gain, qkv_weight, out_weight, layout):
    return sublayer(tokens, norm_gain, qkv_weight, out_weight, layout, spans, lanes)


def solution(mesh):
    placed = (P(("ctx", "fsdp"), None), P(), P(None, "ctx", "fsdp"), P("fsdp", "ctx"), P())
    return jax.shard_map(
        functools.partial(shards, mesh.shape["ctx"], mesh.shape["fsdp"]),
        mesh=mesh, in_specs=placed, out_specs=P(("ctx", "fsdp"), None), check_vma=False,
    )
```

```python
import functools
import math

import jax
import jax.numpy as jnp
from jax import lax
from jax.experimental import pallas as pl
from jax.experimental.pallas import tpu as pltpu
from jax.sharding import PartitionSpec as P

HEAD_DIM = 128
BLK = 128
EPSILON = 1e-05
CAP = 2
MESH = pl.DeviceIdType.MESH


def block_tables(layout, spans):
    me = lax.axis_index("ctx")
    blocks, listed = layout.shape
    own = blocks // spans
    entries = layout.reshape(spans, own, listed)
    home, within = entries // own, entries % own
    mine = home == me
    lowest = jnp.min(jnp.where(mine, within, own - 1), axis=(1, 2))
    highest = jnp.max(jnp.where(mine, within, 0), axis=(1, 2))
    pick = jnp.stack([lowest, highest])
    span = jnp.arange(spans, dtype=jnp.int32)
    rows = jnp.sum(jnp.where(span[:, None, None] == me, entries, 0), axis=0)
    row_home, row_within = rows // own, rows % own
    from_span = row_home[:, :, None] == span
    lows = jnp.min(jnp.where(from_span, row_within[:, :, None], own - 1), axis=(0, 1))
    low = jnp.sum(jnp.where(from_span, lows, 0), axis=2)
    far = own + CAP * row_home + jnp.where(row_within == low, 0, 1)
    listed_slot = jnp.where(row_home == me, row_within, far)
    index = jnp.arange(own, dtype=jnp.int32)
    block = me * own + index
    before = jnp.where(index > 0, index - 1, jnp.where(me > 0, own + CAP * spans, 0))
    slot = jnp.concatenate([index[:, None], before[:, None], listed_slot], axis=1)
    gap = block[:, None] - rows
    before_gap = jnp.where(block > 0, 1, -1)
    reach = jnp.concatenate([jnp.zeros_like(index)[:, None], before_gap[:, None], gap], axis=1) * BLK
    return pick.astype(jnp.int32), slot.astype(jnp.int32), reach.astype(jnp.int32)


def gather(side, eps, enter, tokens, gain, weights, out_weight, rows_all, normed, held, projection, send_t, recv_t, send_w, recv_w, own_sem):
    ctx, lane = lax.axis_index("ctx"), lax.axis_index("fsdp")
    x, y = ctx // side, lax.rem(ctx, side)
    z, core = lane // 2, lax.rem(lane, 2)
    part, width = tokens.shape
    depth = weights.shape[1]
    half, quarter = part // 2, depth // 4

    def shift(at, by):
        return lax.rem(at + by + side, side)

    def along(axis, by):
        if axis == "x":
            return (shift(x, by) * side + y, lane)
        if axis == "y":
            return (x * side + shift(y, by), lane)
        if axis == "z":
            return (ctx, shift(z, by) * 2 + core)
        return (ctx, z * 2 + 1 - core)

    sent = []

    def send_tokens(owner, h, peer, own=False):
        there = rows_all.at[pl.ds(pl.multiple_of(owner * part + h * half, half), half)]
        here = tokens.at[pl.ds(h * half, half)] if own else there
        copy = pltpu.make_async_remote_copy(
            here, there, send_t.at[len([c for c in sent if c[0] == "t"])], recv_t.at[owner, h], device_id=peer, device_id_type=MESH
        )
        copy.start()
        sent.append(("t", copy))

    def wait_tokens(owner, h):
        there = rows_all.at[pl.ds(pl.multiple_of(owner * part + h * half, half), half)]
        pltpu.make_async_remote_copy(
            there, there, send_t.at[0], recv_t.at[owner, h], device_id=along("core", 1), device_id_type=MESH
        ).wait_recv()

    def rows_of(ref, start, count):
        return ref.at[:, pl.ds(start, count)] if len(ref.shape) == 3 else ref.at[pl.ds(start, count)]

    families = ((weights, held), (out_weight, projection))

    def piece_of(owner, p, kind):
        return rows_of(families[kind][1], pl.multiple_of(owner * depth + p * quarter, quarter), quarter)

    def send_weights(owner, p, peer, kind=0, own=False):
        there = piece_of(owner, p, kind)
        here = rows_of(families[kind][0], p * quarter, quarter) if own else there
        copy = pltpu.make_async_remote_copy(
            here, there, send_w.at[kind, len([c for c in sent if c[0] == kind])], recv_w.at[kind, owner, p],
            device_id=peer, device_id_type=MESH,
        )
        copy.start()
        sent.append((kind, copy))

    def wait_weights(owner, p, kind=0):
        piece = piece_of(owner, p, kind)
        pltpu.make_async_remote_copy(
            piece, piece, send_w.at[kind, 0], recv_w.at[kind, owner, p], device_id=along("core", 1), device_id_type=MESH
        ).wait_recv()

    def normalize_rows(owner):
        @pl.loop(0, part // 16)
        def _(n):
            at = pl.ds(pl.multiple_of(owner * part + n * 16, 16), 16)
            features = rows_all[at, :].astype(jnp.float32)
            mean_square = jnp.mean(features * features, axis=-1, keepdims=True)
            normed[at, :] = (features * lax.rsqrt(mean_square + eps) * gain[...]).astype(jnp.bfloat16)

    keep = [
        pltpu.make_async_copy(tokens, rows_all.at[pl.ds(pl.multiple_of(lane * part, part), part)], own_sem.at[0]),
        pltpu.make_async_copy(weights, held.at[:, pl.ds(pl.multiple_of(ctx * depth, depth), depth)], own_sem.at[1]),
        pltpu.make_async_copy(out_weight, projection.at[pl.ds(pl.multiple_of(ctx * depth, depth), depth)], own_sem.at[2]),
    ]
    for copy in keep:
        copy.start()
    enter()

    routes = (("x", "y", 0), ("y", "x", 2))

    def owner_at(axis, by, other=0):
        if axis == "x":
            return shift(x, by) * side + shift(y, other)
        return shift(x, other) * side + shift(y, by)

    right, left, sibling = along("z", 1), along("z", -1), along("core", 1)
    lane_at = lambda by, flip=0: shift(z, by) * 2 + (1 - core if flip else core)
    send_tokens(lane, 0, right, own=True)
    send_tokens(lane, 1, left, own=True)

    def send_own(turn, kind=0):
        for route in routes:
            axis, p = route[turn], route[2]
            send_weights(ctx, p, along(axis, 1), kind, own=True)
            send_weights(ctx, p + 1, along(axis, -1), kind, own=True)
            send_weights(ctx, p + 1, along(axis, 1), kind, own=True)
            send_weights(ctx, p, along(axis, -1), kind, own=True)

    send_own(0)
    send_tokens(lane, 1, right, own=True)
    send_tokens(lane, 0, left, own=True)
    for h in range(2):
        send_tokens(lane, h, sibling, own=True)
    send_own(1)
    for copy in keep:
        copy.wait()
    normalize_rows(lane)

    def spread(owner, p, axis, kind):
        send_weights(owner, p, along(axis, 1), kind)
        send_weights(owner, p, along(axis, -1), kind)

    def turn_corner(kind=0):
        for first, second, p in routes:
            wait_weights(owner_at(first, -1), p, kind)
            send_weights(owner_at(first, -1), p, along(first, 1), kind)
            wait_weights(owner_at(first, 1), p + 1, kind)
            send_weights(owner_at(first, 1), p + 1, along(first, -1), kind)
        for first, second, p in routes:
            spread(owner_at(first, -1), p, second, kind)
            spread(owner_at(first, 1), p + 1, second, kind)
        for first, second, p in routes:
            wait_weights(owner_at(first, -1), p + 1, kind)
            spread(owner_at(first, -1), p + 1, second, kind)
            wait_weights(owner_at(first, 1), p, kind)
            spread(owner_at(first, 1), p, second, kind)
        for first, second, p in routes:
            for q in (p, p + 1):
                wait_weights(owner_at(first, 2), q, kind)
                spread(owner_at(first, 2), q, second, kind)

    def relay(by, kind=0):
        for first, second, p in routes:
            owner = owner_at(first, by, -1)
            wait_weights(owner, p, kind)
            send_weights(owner, p, along(second, 1), kind)
            owner = owner_at(first, by, 1)
            wait_weights(owner, p + 1, kind)
            send_weights(owner, p + 1, along(second, -1), kind)

    def finish(kind=0):
        for first, second, p in routes:
            for by in (0, -1, 1, 2):
                wait_weights(owner_at(first, by, -1), p + 1, kind)
                wait_weights(owner_at(first, by, 1), p, kind)
                wait_weights(owner_at(first, by, 2), p, kind)
                wait_weights(owner_at(first, by, 2), p + 1, kind)

    turn_corner()
    relay(0)
    wait_tokens(lane_at(-1), 0)
    send_tokens(lane_at(-1), 0, right)
    send_tokens(lane_at(-1), 0, sibling)
    wait_tokens(lane_at(1), 1)
    send_tokens(lane_at(1), 1, left)
    send_tokens(lane_at(1), 1, sibling)
    relay(-1)
    relay(1)
    for h in range(2):
        wait_tokens(lane_at(0, 1), h)
    normalize_rows(lane_at(0, 1))
    wait_tokens(lane_at(-1), 1)
    send_tokens(lane_at(-1), 1, sibling)
    wait_tokens(lane_at(1), 0)
    send_tokens(lane_at(1), 0, sibling)
    normalize_rows(lane_at(-1))
    normalize_rows(lane_at(1))
    relay(2)
    send_own(0, 1)
    send_own(1, 1)
    for by in (-1, 1):
        for h in range(2):
            wait_tokens(lane_at(by, 1), h)
        normalize_rows(lane_at(by, 1))
    for h in range(2):
        wait_tokens(lane_at(2), h)
        send_tokens(lane_at(2), h, sibling)
    normalize_rows(lane_at(2))
    finish()
    turn_corner(1)
    for h in range(2):
        wait_tokens(lane_at(2, 1), h)
    normalize_rows(lane_at(2, 1))

    return sent, lambda *steps: [relay(by, 1) for by in steps], lambda: finish(1)


def attend_kernel(
    side, spans, slots, pick, slot, reach, tokens, gain, weights, out_weight, out, rows_all, normed, held, projection, projected,
    kpool, vpool, kstage, vstage, scores, attended, partial, crossed, packed, hop, final,
    send_t, recv_t, send_w, recv_w, own_sem, send_sem, recv_sem, cross_sem, sum_send, sum_recv,
):
    me, lane = lax.axis_index("ctx"), lax.axis_index("fsdp")
    q, k, v = (projected.at[which] for which in range(3))
    z, core = lane // 2, lax.rem(lane, 2)
    chips = 4
    pieces, wide = spans, held.shape[2]
    half = pieces // 2
    right = (me, lax.rem(z + 1, chips) * 2 + core)
    left = (me, lax.rem(z + chips - 1, chips) * 2 + core)
    sibling = (me, z * 2 + 1 - core)
    own = q.shape[0]
    width = q.shape[2]
    heads = width // HEAD_DIM
    barrier = pltpu.get_barrier_semaphore()

    @pl.loop(1, spans)
    def _(step):
        peer = lax.rem(me + step, spans)
        pl.semaphore_signal(barrier, inc=1, device_id=(peer, lane), device_id_type=MESH)

    for peer in (right, left, sibling):
        pl.semaphore_signal(barrier, inc=1, device_id=peer, device_id_type=MESH)

    sent, relay_projection, finish_projection = gather(
        side, EPSILON, lambda: pl.semaphore_wait(barrier, spans + 2), tokens, gain, weights, out_weight,
        rows_all, normed, held, projection, send_t, recv_t, send_w, recv_w, own_sem,
    )
    tile = 2 * BLK

    def project(which):
        @pl.loop(0, normed.shape[0] // tile)
        def _(n):
            rows = normed[pl.ds(pl.multiple_of(n * tile, tile), tile), :]
            product = jnp.dot(rows, held[which], preferred_element_type=jnp.float32)
            projected[which, pl.ds(2 * n, 2)] = product.astype(jnp.bfloat16).reshape(2, BLK, width)

    x, y = me // side, lax.rem(me, side)
    exchanged = ((k, kstage, kpool), (v, vstage, vpool))

    def listed(j, src, dst):
        _, stage, pool = exchanged[j]
        return pltpu.make_async_remote_copy(
            stage.at[pl.ds(CAP * dst, CAP)], pool.at[pl.ds(own + CAP * src, CAP)],
            send_sem.at[dst, j], recv_sem.at[src, j], device_id=(dst, lane), device_id_type=MESH,
        )

    def previous(j, dst):
        mine, _, pool = exchanged[j]
        return pltpu.make_async_remote_copy(
            mine.at[own - 1], pool.at[own + CAP * spans],
            send_sem.at[spans, j], recv_sem.at[spans, j], device_id=(dst, lane), device_id_type=MESH,
        )

    def exchange(j):
        mine, stage, pool = exchanged[j]
        keep = pltpu.make_async_copy(mine, pool.at[pl.ds(0, own)], own_sem.at[j])
        keep.start()

        @pl.loop(0, spans)
        def _(dst):
            for which in range(CAP):
                stage[CAP * dst + which] = mine[pick[which, dst]]

        for by in (2, 3, 1, 0):

            @pl.loop(0, side)
            def _(step):
                dst = (x + by) * side + lax.rem(y + step, side)

                @pl.when((x + by < side) & (dst > me))
                def _():
                    listed(j, me, dst).start()

        @pl.when(me < spans - 1)
        def _():
            previous(j, me + 1).start()

        return keep

    project(1)
    relay_projection(0, -1, 1)
    keep = [exchange(0)]
    project(2)
    relay_projection(2)
    keep.append(exchange(1))
    project(0)
    finish_projection()
    for copy in keep:
        copy.wait()

    @pl.when(me > 0)
    def _():
        for j in range(2):
            previous(j, me).wait_recv()

    @pl.loop(1, spans)
    def _(step):
        @pl.when(me >= step)
        def _():
            for j in range(2):
                listed(j, me - step, me).wait_recv()

    column = lax.broadcasted_iota(jnp.int32, (BLK, 2 * BLK), 1)
    late = column >= BLK
    offset = lax.rem(column, BLK) - lax.broadcasted_iota(jnp.int32, (BLK, 2 * BLK), 0)

    def attend(b, at):
        for head in range(heads):
            columns = pl.ds(head * HEAD_DIM, HEAD_DIM)
            query = q[b, :, columns]
            pair = lambda pool, n: jnp.concatenate(
                [pool[slot[b, n], :, columns], pool[slot[b, n + 1], :, columns]], axis=0
            )
            top = jnp.full((BLK, 2 * BLK), -1e30, jnp.float32)
            for n in range(0, slots, 2):
                part = lax.dot_general(
                    query, pair(kpool, n), (((1,), (1,)), ((), ())), preferred_element_type=jnp.float32
                )
                limit = jnp.where(late, reach[b, n + 1], reach[b, n])
                part = jnp.where(offset <= limit, part, -1e30)
                scores[n // 2] = part
                top = jnp.maximum(top, part)
            top = jnp.max(top, axis=1, keepdims=True)
            total = jnp.zeros((BLK, 2 * BLK), jnp.float32)
            blended = jnp.zeros((BLK, HEAD_DIM), jnp.float32)
            for n in range(0, slots, 2):
                terms = jnp.exp((scores[n // 2] - top) * HEAD_DIM**-0.5)
                total += terms
                blended += jnp.dot(terms.astype(jnp.bfloat16), pair(vpool, n), preferred_element_type=jnp.float32)
            total = jnp.sum(total, axis=1, keepdims=True)
            attended[at, :, columns] = (blended / total).astype(jnp.bfloat16)

    def cross(g):
        return pltpu.make_async_remote_copy(
            partial.at[g, 0], crossed.at[g], cross_sem.at[0, g], cross_sem.at[1, g], device_id=sibling, device_id_type=MESH
        )

    def travel(n, source, target, peer):
        return pltpu.make_async_remote_copy(
            source, target, sum_send.at[n], sum_recv.at[n], device_id=peer, device_id_type=MESH
        )

    first, second = pl.ds(0, half), pl.ds(half, half)
    travels = [
        travel(0, packed.at[0, first], hop.at[0], right),
        travel(1, packed.at[0, second], hop.at[1], left),
        travel(2, packed.at[1, second], final.at[0, second], right),
        travel(3, packed.at[1, first], final.at[0, first], right),
        travel(4, packed.at[2, first], final.at[1, first], left),
        travel(5, packed.at[2, second], final.at[1, second], left),
    ]

    def add(g, low, more=None):
        @pl.loop(0, half)
        def _(n):
            term = partial[g, 1, low + n].astype(jnp.float32) + crossed[g, low + n].astype(jnp.float32)
            if more is not None:
                term += hop[more, n].astype(jnp.float32)
            packed[g, low + n] = term.astype(jnp.bfloat16)

    for g, steps in enumerate((2, 1, -1, 0)):
        chip = lax.rem(z + steps + chips, chips)

        @pl.loop(0, 2)
        def _(turn):
            attend(chip * 2 + lax.rem(core + 1 + turn, 2), turn)

            @pl.loop(0, pieces)
            def _(n):
                partial[g, turn, n] = jnp.dot(
                    attended[turn], projection[pl.ds(pl.multiple_of(n * width, width), width), :], preferred_element_type=jnp.float32
                ).astype(jnp.bfloat16)

            @pl.when(turn == 0)
            def _():
                cross(g).start()

        cross(g).wait_recv()
        if g == 0:
            add(0, 0)
            travels[0].start()
            add(0, half)
            travels[1].start()
        elif g == 1:
            add(1, half)
            travels[2].start()
        elif g == 2:
            add(2, 0)
            travels[4].start()
            travels[0].wait_recv()
            add(1, 0, 0)
            travels[3].start()
            travels[1].wait_recv()
            add(2, half, 1)
            travels[5].start()

    for low, waits in ((half, (2, 5)), (0, (3, 4))):
        for n in waits:
            travels[n].wait_recv()

        @pl.loop(0, half)
        def _(n):
            at = low + n
            term = partial[3, 1, at].astype(jnp.float32) + crossed[3, at].astype(jnp.float32)
            term += final[0, at].astype(jnp.float32) + final[1, at].astype(jnp.float32)
            out[:, pl.ds(pl.multiple_of(at * wide, wide), wide)] = term.astype(jnp.bfloat16)

    for g in range(chips):
        cross(g).wait_send()
    for copy in travels:
        copy.wait_send()

    @pl.when(me < spans - 1)
    def _():
        for j in range(2):
            previous(j, me + 1).wait_send()

    @pl.loop(1, spans)
    def _(step):
        @pl.when(me + step < spans)
        def _():
            for j in range(2):
                listed(j, me, me + step).wait_send()
    for _, copy in sent:
        copy.wait_send()


def sublayer(tokens, norm_gain, qkv_weight, out_weight, layout, spans, lanes):
    part, features = tokens.shape
    width = qkv_weight.shape[2]
    rows = lanes * part
    slots = 2 + layout.shape[1]
    pick, slot, reach = block_tables(layout, spans)
    own = rows // BLK
    pool = own + CAP * spans + 1
    whole = (spans, BLK, out_weight.shape[1])
    smem = pl.BlockSpec(memory_space=pltpu.SMEM)
    vmem = pl.BlockSpec(memory_space=pltpu.VMEM)
    bf16 = lambda *shape: pltpu.VMEM(shape, jnp.bfloat16)
    dma = lambda *shape: pltpu.SemaphoreType.DMA(shape)
    side = math.isqrt(spans)
    return pl.pallas_call(
        functools.partial(attend_kernel, side, spans, slots),
        out_shape=jax.ShapeDtypeStruct((BLK, features), jnp.bfloat16),
        in_specs=[smem] * 3 + [vmem] * 4,
        out_specs=vmem,
        scratch_shapes=[
            bf16(rows, features), bf16(rows, features), bf16(3, features, width), bf16(features, width),
            bf16(3, own, BLK, width),
            bf16(pool, BLK, width), bf16(pool, BLK, width), bf16(spans * CAP, BLK, width), bf16(spans * CAP, BLK, width),
            pltpu.VMEM((slots // 2, BLK, 2 * BLK), jnp.float32), bf16(2, BLK, width),
            bf16(4, 2, *whole), bf16(4, *whole), bf16(3, *whole), bf16(2, spans // 2, *whole[1:]), bf16(2, *whole),
            dma(14), dma(lanes, 2), dma(2, 60), dma(2, spans, 4), dma(3),
            dma(spans + 1, 2), dma(spans + 1, 2), dma(2, 4), dma(6), dma(6),
        ],
        compiler_params=pltpu.CompilerParams(
            collective_id=0, has_side_effects=True, vmem_limit_bytes=67043328
        ),
    )(pick, slot, reach, tokens, norm_gain[None, :], qkv_weight, out_weight)


def shards(spans, lanes, tokens, norm_gain, qkv_weight, out_weight, layout):
    return sublayer(tokens, norm_gain, qkv_weight, out_weight, layout, spans, lanes)


def solution(mesh):
    placed = (P(("ctx", "fsdp"), None), P(), P(None, "ctx", "fsdp"), P("fsdp", "ctx"), P())
    return jax.shard_map(
        functools.partial(shards, mesh.shape["ctx"], mesh.shape["fsdp"]),
        mesh=mesh, in_specs=placed, out_specs=P(("ctx", "fsdp"), None), check_vma=False,
    )
```
